256 devices in a mesh: tm: 16 (over y, z_hi), chan: 16 (over z_lo, x, core).
Axes of the slice: x: 4, y: 4, z: 8 (z_hi: 4, z_lo: 2; z = z_hi * 2 + z_lo), core: 2. Of those that a mesh axis runs over, the one named last changes fastest.
Arguments:
- raw_strain: bfloat16 [4096, 81920], P('chan', 'tm'), may hold values from -48 to 48
- fir_taps: float32 [128], replicated, may hold values from -0.5 to 0.5
- source_channels: int32 [256], replicated, may hold values from 0 to 4095, as said below
- live_counts: int32 [256], P(('chan', 'tm')), may hold values from 8 to 16, as said below
Outputs:
- correlations: float32 [256, 4096, 384], P(None, ('chan', 'tm'))
The draws below stay inside these ranges and needn't reach their ends.
Inputs may be any that keep to these rules, and one draw needn't show every extreme that they name: `source_channels`: the virtual sources are distinct live channels; at most 2 of them lie in one aligned block of 16 channels, and some block holds exactly 2. `live_counts`: some block has all 16 channels live and some has exactly half of them.
All inputs are finite; a program needn't handle non-finite values.
Results may differ from the reference program's by a relative error of at most 0.015.
Values may be sent and summed in bfloat16 or wider, within the bound.
A program may use at most 128 MiB of HBM per device.

```python
import math
import jax
import jax.numpy as jnp
from jax import lax

TAPS = 128
DECIM = 10
SEG = 1024
BAND = 64
LAGH = 192
SRC_DEV = 1
CH_DEV = 16
NCH = 4096
NBLK = 256
NTR = 81920
NSEG = 8
SRC = 256


def draw_raw_strain(key, part):
    noise_key, chan_key, env_key = jax.random.split(key, 3)
    env_count = NTR // 64
    noise_field = jnp.clip(jax.random.normal(noise_key, (NCH, NTR), jnp.float32), -6.0, 6.0)
    chan_scale = jnp.exp(jax.random.uniform(chan_key, (NCH, 1), jnp.float32, math.log(0.3), math.log(3.0)))
    envelope = jnp.exp(jax.random.uniform(env_key, (1, env_count), jnp.float32, math.log(0.5), math.log(2.0)))
    envelope = jnp.repeat(envelope, 64, axis=1)
    return (noise_field * chan_scale * envelope).astype(jnp.bfloat16)


def layout_draw(key):
    base = jax.random.fold_in(key, 7)
    count_key, order_key, pair_key, score_key, shuffle_key = jax.random.split(base, 5)
    counts = jax.random.randint(count_key, (NBLK,), CH_DEV // 2, CH_DEV + 1)
    block_order = jax.random.permutation(order_key, NBLK)
    counts = counts.at[block_order[0]].set(CH_DEV).at[block_order[1]].set(CH_DEV // 2)
    pair_shift = jax.random.randint(pair_key, (NBLK // 2,), 0, SRC_DEV + 1)
    pair_shift = pair_shift.at[0].set(SRC_DEV)
    first_half = block_order[0::2]
    second_half = block_order[1::2]
    per_block = jnp.zeros((NBLK,), jnp.int32)
    per_block = per_block.at[first_half].set(SRC_DEV + pair_shift).at[second_half].set(SRC_DEV - pair_shift)
    positions = jnp.arange(CH_DEV, dtype=jnp.int32)
    scores = jax.random.randint(score_key, (NBLK, CH_DEV), 0, 1 << 16) * CH_DEV + positions[None, :]
    is_live = positions[None, :] < counts[:, None]
    scores = jnp.where(is_live, scores, (1 << 24) + positions[None, :])
    chosen_spots = jnp.argsort(scores, axis=1, stable=True)[:, :2 * SRC_DEV].astype(jnp.int32)
    block_index = jnp.arange(NBLK, dtype=jnp.int32)
    candidate = (block_index[:, None] * CH_DEV + chosen_spots).reshape(-1)
    is_valid = (jnp.arange(2 * SRC_DEV, dtype=jnp.int32)[None, :] < per_block[:, None]).reshape(-1)
    keep_order = jnp.argsort(jnp.where(is_valid, 0, 1), stable=True)[:SRC]
    selected = candidate[keep_order]
    shuffle = jax.random.permutation(shuffle_key, SRC)
    return (counts.astype(jnp.int32), selected[shuffle].astype(jnp.int32))


def draw_source_channels(key, part):
    return layout_draw(key)[1]


def draw_live_counts(key, part):
    return layout_draw(key)[0]


def gaussian(own_key, shape, width, reach, kind=jnp.bfloat16):
    result = width * jax.random.normal(own_key, shape, jnp.float32)
    return jnp.clip(result, min=-reach, max=reach).astype(kind)


def setup_inputs(seed: int = 0) -> dict:
    key_of = jax.random.split(jax.random.key(seed), 5)
    raw_strain = draw_raw_strain(jax.random.fold_in(key_of[4], 71), 0)
    fir_taps = gaussian(key_of[1], (TAPS,), TAPS ** -0.5, 0.5, jnp.float32)
    source_channels = draw_source_channels(jax.random.fold_in(key_of[4], 71), 0)
    live_counts = draw_live_counts(jax.random.fold_in(key_of[4], 71), 0)
    return dict(raw_strain=raw_strain, fir_taps=fir_taps, source_channels=source_channels, live_counts=live_counts)


whiten_eps = 1e-06

def whiten_rows(traces):
    rows = traces.shape[0]
    half_len = SEG // 2
    segments = traces.astype(jnp.float32).reshape(rows, NSEG, SEG)
    spectrum = jnp.fft.rfft(segments, axis=-1)[..., :half_len]
    real_part = jnp.real(spectrum)
    imag_part = jnp.imag(spectrum)
    band_power = (real_part * real_part + imag_part * imag_part).reshape(rows, NSEG, half_len // BAND, BAND)
    band_scale = 1.0 / jnp.sqrt(lax.optimization_barrier(jnp.mean(band_power, axis=-1)) + whiten_eps)
    band_scale = jnp.repeat(band_scale, BAND, axis=-1)
    return jnp.concatenate([real_part * band_scale, imag_part * band_scale], axis=-1).astype(jnp.bfloat16)

def reference(raw_strain, fir_taps, source_channels, live_counts):
    block_ids = jnp.arange(NBLK, dtype=jnp.int32)
    half_len = SEG // 2

    def prepare(block_id):
        rows = lax.dynamic_slice_in_dim(raw_strain, block_id * CH_DEV, CH_DEV, 0).astype(jnp.float32)
        kernel = jnp.flip(fir_taps).astype(rows.dtype)[None, None, :]
        filtered = lax.conv_general_dilated(rows[:, None, :], kernel, (DECIM,), [(TAPS - 1, 0)], precision=lax.Precision.HIGHEST)[:, 0, :]
        decimated = filtered.astype(jnp.bfloat16)
        is_live = jnp.arange(CH_DEV, dtype=jnp.int32) < live_counts[block_id]
        traces = jnp.where(is_live[:, None], decimated, jnp.zeros_like(decimated))
        return whiten_rows(traces)
    whitened = lax.map(prepare, block_ids).reshape(NCH, NSEG, SEG)
    sources = jnp.take(whitened, source_channels, axis=0).astype(jnp.float32)
    src_re = sources[..., :half_len]
    src_im = sources[..., half_len:]
    lag_index = jnp.mod(jnp.arange(-LAGH, LAGH, dtype=jnp.int32), SEG)
    factor = math.sqrt(SEG / NSEG)
    highest = lax.Precision.HIGHEST

    def correlate(block_id):
        local = lax.dynamic_slice_in_dim(whitened, block_id * CH_DEV, CH_DEV, 0).astype(jnp.float32)
        loc_re = local[..., :half_len]
        loc_im = local[..., half_len:]
        cross_re = jnp.einsum('csk,nsk->nck', loc_re, src_re, precision=highest) + jnp.einsum('csk,nsk->nck', loc_im, src_im, precision=highest)
        cross_im = jnp.einsum('csk,nsk->nck', loc_im, src_re, precision=highest) - jnp.einsum('csk,nsk->nck', loc_re, src_im, precision=highest)
        spectrum = cross_re + 1j * cross_im
        spectrum = jnp.pad(spectrum, ((0, 0), (0, 0), (0, 1)))
        full_lags = jnp.fft.irfft(spectrum, n=SEG, axis=-1)
        return jnp.take(full_lags, lag_index, axis=-1) * factor
    blocks = lax.map(correlate, block_ids)
    return jnp.transpose(blocks, (1, 0, 2, 3)).reshape(SRC, NCH, 2 * LAGH).astype(jnp.float32)
```

```python
import functools
import math

import jax
import jax.numpy as jnp
import numpy as np
from jax import lax
from jax.experimental import pallas as pl
from jax.experimental.pallas import tpu as pltpu
from jax.sharding import PartitionSpec as P

NX, NY, NZ, NC = 4, 4, 8, 2
TM, CHAN = 16, 16
DECIM, SEG, BAND, LAGH = 10, 1024, 64, 192
NSEG = 8
HALF = SEG // 2
SRC = 256
SLOTS = 512
EPS = 1e-06
MESH = pl.DeviceIdType.MESH
F32, BF16 = jnp.float32, jnp.bfloat16
TAPS = 128
REACH = 1408
KG = HALF // BAND
PARTS = ((0, 2), (2, 3), (5, 3))


def dot(a, b):
    return jnp.dot(a, b, preferred_element_type=F32)


def hi_lo(table):
    hi = table.astype(np.float32).astype(jnp.bfloat16)
    lo = (table - hi.astype(np.float64)).astype(np.float32).astype(jnp.bfloat16)
    return hi, lo


def dft_table():
    n = np.arange(HALF)[:, None]
    k = np.arange(HALF)[None, :]
    phase = (n * k % SEG) * (2.0 * np.pi / SEG)
    both = np.stack([np.cos(phase), -np.sin(phase)], axis=1).reshape(HALF, 2, KG, BAND)
    table = both.transpose(0, 2, 1, 3).reshape(HALF, SEG)
    return np.concatenate(hi_lo(table), axis=1)


def lag_table():
    k = np.arange(HALF)[:, None]
    t = np.arange(-LAGH, LAGH)[None, :]
    phase = (k * t % SEG) * (2.0 * np.pi / SEG)
    weight = np.where(k == 0, 1.0, 2.0) * (math.sqrt(SEG / NSEG) / SEG)
    both = np.stack([weight * np.cos(phase), -weight * np.sin(phase)], axis=0)
    table = both.reshape(2, KG, BAND, 2 * LAGH).transpose(1, 0, 2, 3).reshape(SEG, 2 * LAGH)
    return table.astype(np.float32).astype(jnp.bfloat16)


def whiten(spec):
    bands = []
    for band in range(KG):
        block = spec[:, band * 128 : (band + 1) * 128]
        power = jnp.sum(block * block, axis=1, keepdims=True) * (1.0 / BAND)
        bands.append(block * lax.rsqrt(power + EPS))
    return jnp.concatenate(bands, axis=1).astype(BF16)


def odd_sign(rows):
    lane = lax.broadcasted_iota(jnp.int32, (rows, SEG), 1)
    return (1 - 2 * lax.rem(lane, 2)).astype(F32)


def place(x, y, z, core):
    return (y * 4 + z // 2, lax.rem(z, 2) * 8 + x * 2 + core)


def gather_part(buf, semaphores, core, order, step_dir, sends, first):
    send_sem, recv_sem = semaphores
    count = 0
    for stage, (me, size, chunk, device) in enumerate(order):
        far, near = size // 2, size - 1 - size // 2

        def index(offset):
            return lax.rem(me + step_dir * offset + size, size)

        def send(src, dst, to, number):
            copy = pltpu.make_async_remote_copy(
                src_ref=src,
                dst_ref=dst,
                send_sem=send_sem.at[number],
                recv_sem=recv_sem.at[number],
                device_id=device(index(to)),
                device_id_type=MESH,
            )
            copy.start()
            sends.append(copy)

        def arrived(offset, number):
            block = chunk(index(offset))
            pltpu.make_async_remote_copy(
                src_ref=block,
                dst_ref=block,
                send_sem=send_sem.at[number],
                recv_sem=recv_sem.at[number],
                device_id=device(index(1)),
                device_id_type=MESH,
            ).wait_recv()
            return block

        own = chunk(me)
        start = first if stage == 0 else own
        send(start, own, 1, count)
        send(start, own, -1, count + far)
        last = stage == len(order) - 1
        if last:
            yield own
        for hop in range(1, far + 1):
            yield None
            block = arrived(-hop, count + hop - 1)
            if hop < far:
                send(block, block, 1, count + hop)
            if last:
                yield block
            if hop <= near:
                block = arrived(hop, count + far + hop - 1)
                if hop < near:
                    send(block, block, -1, count + far + hop)
                if last:
                    yield block
        count += far + near


def gather_kernel(
    raw_hbm, rev_ref, src_ref, live_ref, table_hbm,
    a_ref, b_ref, c_ref, white_ref,
    raw_v, tap_v, dec_v, sel_v, pair_v, trace_v, table_v, own_v,
    load_sem, table_sem, halo_sem, pair_sem, trace_send, trace_recv,
    a_send, a_recv, b_send, b_recv, c_send, c_recv, own_sem, twin_send, twin_recv,
):
    tm = lax.axis_index("tm")
    chan = lax.axis_index("chan")
    y, z_hi = tm // 4, lax.rem(tm, 4)
    z_lo, x, core = chan // 8, lax.rem(chan, 8) // 2, lax.rem(chan, 2)
    z = z_hi * 2 + z_lo
    direction = 1 - 2 * core
    half = lax.rem(tm, 2)

    def remote(src, dst, sems, device):
        return pltpu.make_async_remote_copy(
            src_ref=src, dst_ref=dst, send_sem=sems[0], recv_sem=sems[1], device_id=device, device_id_type=MESH
        )

    loads = []
    for part in range(4):
        loads.append(
            pltpu.make_async_copy(
                raw_hbm.at[:, part * 1280 : (part + 1) * 1280],
                raw_v.at[:, 128 + part * 1280 : 128 + (part + 1) * 1280],
                load_sem.at[part],
            )
        )
        loads[-1].start()
    table_load = pltpu.make_async_copy(table_hbm, table_v, table_sem)
    table_load.start()

    barrier = pltpu.get_barrier_semaphore()
    peers = [(lax.rem(tm + step, TM), chan) for step in range(1, TM)]
    for to_x in (1, 3):
        peers.append(place(lax.rem(x + to_x, NX), y, z, core))
    for to_z in (1, 7):
        peers.append(place(x, y, lax.rem(z + to_z, NZ), core))
    twin = place(x, y, z, 1 - core)
    peers.append(twin)
    for peer in peers:
        pl.semaphore_signal(barrier, inc=1, device_id=peer, device_id_type=MESH)
    pl.semaphore_wait(barrier, len(peers))

    halo = remote(
        raw_hbm.at[:, 4992:5120], raw_v.at[:, 0:128], (halo_sem.at[0], halo_sem.at[1]), (lax.rem(tm + 1, TM), chan)
    )
    halo.start()

    base = pltpu.roll(jnp.broadcast_to(rev_ref[...], (8, 384)), 0, 1, stride=DECIM, stride_axis=0)
    for group in range(8):
        rows = []
        for octet in (2 * group, 2 * group + 1):
            at, turn = divmod(octet * 8 * DECIM, 128)
            piece = pltpu.roll(base, turn, 1) if turn else base
            blocks = [jnp.zeros((8, 128), F32)] * (REACH // 128)
            for number in range(min(3, REACH // 128 - at)):
                blocks[at + number] = piece[:, number * 128 : (number + 1) * 128]
            rows.append(jnp.concatenate(blocks, axis=1))
        band = jnp.concatenate(rows, axis=0)
        band_hi = band.astype(BF16)
        tap_v[group * 16 : group * 16 + 16, :] = band_hi
        tap_v[128 + group * 16 : 128 + group * 16 + 16, :] = (band - band_hi.astype(F32)).astype(BF16)

    src = src_ref[...].astype(F32)
    src_col = jnp.transpose(jnp.broadcast_to(src, (SRC, SRC)))
    lane = lax.broadcasted_iota(jnp.int32, (SRC, SRC), 1)
    row = lax.broadcasted_iota(jnp.int32, (SRC, SRC), 0)
    hit = jnp.where(src_col == (lane + chan * 256).astype(F32), 1.0, 0.0)
    is_src = jnp.sum(hit, axis=0, keepdims=True)
    earlier = jnp.where((row // 16 == lane // 16) & (row < lane), 1.0, 0.0)
    rank = dot(jnp.broadcast_to(is_src, (16, SRC)).astype(BF16), earlier.astype(BF16))[0:1, :]
    pick_row = lax.broadcasted_iota(jnp.int32, (32, SRC), 0)
    pick_lane = lax.broadcasted_iota(jnp.int32, (32, SRC), 1)
    pick = jnp.where(
        (pick_row // 2 == pick_lane // 16) & (lax.rem(pick_row, 2).astype(F32) == rank) & (is_src > 0.5), 1.0, 0.0
    ).astype(BF16)

    for part in (1, 2, 3, 0):
        if part == 1:
            loads[0].wait()
        if part:
            loads[part].wait()
        else:
            halo.wait()

            @pl.when(tm == 0)
            def _():
                raw_v[:, 0:128] = jnp.zeros((256, 128), BF16)

        both = lax.dot_general(
            raw_v[:, part * 1280 : part * 1280 + REACH],
            tap_v[...],
            (((1,), (1,)), ((), ())),
            preferred_element_type=F32,
        )
        dec_v[:, part * 128 : (part + 1) * 128] = (both[:, 0:128] + both[:, 128:256]).astype(BF16)

    picked = dot(pick, dec_v[...]).astype(BF16)
    sel_v[0] = picked[0:16]
    sel_v[1] = picked[16:32]
    pair = remote(
        sel_v.at[1 - half], pair_v, (pair_sem.at[0], pair_sem.at[1]), (tm + 1 - 2 * half, chan)
    )
    pair.start()

    traces = []
    for step in range(1, TM):
        to = lax.rem(tm + step, TM)
        copy = remote(
            dec_v.at[pl.ds(pl.multiple_of(to * 16, 16), 16), :],
            trace_v.at[tm],
            (trace_send.at[step - 1], trace_recv.at[step - 1]),
            (to, chan),
        )
        copy.start()
        traces.append(copy)
    trace_v[tm] = dec_v[pl.ds(pl.multiple_of(tm * 16, 16), 16), :]

    table_load.wait()
    pair.wait()
    spec = dot(jnp.concatenate([sel_v[half], pair_v[...]], axis=0), table_v[...])
    mine = spec[0:16, 0:SEG] + spec[0:16, SEG:]
    other = spec[16:32, 0:SEG] + spec[16:32, SEG:]
    is_first = half == 0
    sign = odd_sign(16)
    own_v[...] = whiten(jnp.where(is_first, mine, other) + sign * jnp.where(is_first, other, mine))

    def part_order(buf, axes):
        sizes = {"x": NX, "y": NY, "z": NZ}
        at = {"x": x, "y": y, "z": z}
        order = []
        for number, axis in enumerate(axes):
            lead = [at[a] for a in reversed(axes[number + 1 :])]

            def chunk(index, lead=lead):
                return buf.at[(core, *lead, index)]

            def device(index, axis=axis):
                where = dict(at)
                where[axis] = index
                return place(where["x"], where["y"], where["z"], core)

            order.append((at[axis], sizes[axis], chunk, device))
        return order

    sends = []
    routines = []
    own_copies = []
    bufs = ((a_ref, "xyz", a_send, a_recv), (b_ref, "yzx", b_send, b_recv), (c_ref, "zxy", c_send, c_recv))
    for number, (buf, axes, send_sem, recv_sem) in enumerate(bufs):
        begin, bands = PARTS[number]
        first = own_v.at[:, begin * 128 : (begin + bands) * 128]
        at = {"x": x, "y": y, "z": z}
        slot = buf.at[(core, *(at[a] for a in reversed(axes)))]
        copy = pltpu.make_async_copy(first, slot, own_sem.at[number])
        copy.start()
        own_copies.append(copy)
        order = part_order(buf, axes)
        routines.append(gather_part(buf, (send_sem, recv_sem), core, order, direction, sends, first))

    twins = []

    def to_twin(block):
        number = len(twins)
        copy = remote(block, block, (twin_send.at[number], twin_recv.at[number]), twin)
        copy.start()
        twins.append(copy)

    live = list(routines)
    round_number = 0
    while live:
        for routine in list(live):
            while True:
                try:
                    block = next(routine)
                except StopIteration:
                    live.remove(routine)
                    break
                if block is None:
                    break
                to_twin(block)
        if round_number == 0:
            for copy in own_copies:
                copy.wait()
            for copy in traces:
                copy.wait()
            rows = lax.broadcasted_iota(jnp.int32, (256, HALF), 0)
            alive = lax.rem(rows, 16) < live_ref[0]
            flat = trace_v[...].reshape(256, HALF)
            spec = dot(jnp.where(alive, flat, jnp.zeros_like(flat)), table_v[...])
            for seg in range(NSEG):
                low = spec[seg * 32 : seg * 32 + 16]
                high = spec[seg * 32 + 16 : seg * 32 + 32]
                full = low[:, 0:SEG] + low[:, SEG:] + sign * (high[:, 0:SEG] + high[:, SEG:])
                white = whiten(full).astype(F32)
                for band in range(KG):
                    white_ref[band, pl.ds(seg, 16, stride=NSEG), :] = white[:, band * 128 : (band + 1) * 128]
        round_number += 1
    for copy in sends:
        copy.wait_send()
    for copy in twins:
        copy.wait()


def correlate_kernel(src_ref, white_ref, a_ref, b_ref, c_ref, lag_ref, out_hbm, all_v, weight_v, cross_v, out_v, out_sem):
    src = src_ref[...].astype(F32)
    src_row = jnp.broadcast_to(src, (SRC, SRC))
    src_col = jnp.transpose(src_row)
    row_block = jnp.floor(src_row * (1.0 / 16))
    col_block = jnp.floor(src_col * (1.0 / 16))
    before = jnp.where((row_block == col_block) & (src_row < src_col), 1.0, 0.0)
    rank = jnp.sum(before, axis=1, keepdims=True).astype(jnp.int32)
    block = col_block[:, 0:1].astype(jnp.int32)
    chan = block // 16
    local = lax.rem(block, 16)
    run = (local // 8) * 2 + chan // 8
    slot = 2 * lax.rem(local, 8) + rank
    where = run * 128 + lax.rem(chan, 8) * 16 + slot
    pick = jnp.where(where == lax.broadcasted_iota(jnp.int32, (SRC, SLOTS), 1), 1.0, 0.0).astype(BF16)
    for seg in range(NSEG):
        y, run0 = seg // 2, (seg % 2) * 4
        at = [(x, y, z, core) for z in range(run0, run0 + 4) for x in range(NX) for core in range(NC)]
        pieces = (
            [a_ref[core, z, y, x] for x, y, z, core in at],
            [b_ref[core, x, z, y] for x, y, z, core in at],
            [c_ref[core, y, x, z] for x, y, z, core in at],
        )
        for number, (begin, bands) in enumerate(PARTS):
            rows = dot(pick, jnp.concatenate(pieces[number], axis=0)).astype(BF16)
            for band in range(bands):
                lane = ((begin + band) * NSEG + seg) * 128
                all_v[:, lane : lane + 128] = rows[:, band * 128 : (band + 1) * 128]

    half = BAND
    row = lax.broadcasted_iota(jnp.int32, (half, 128), 0)
    lane = lax.broadcasted_iota(jnp.int32, (half, 128), 1)
    same = row == lax.rem(lane, half)
    sign = jnp.where(lane[0:1] < half, 1.0, -1.0)

    def copies(which):
        return [
            pltpu.make_async_copy(
                out_v.at[which, part].reshape(SRC, 8, 128),
                out_hbm.at[:, which * 8 : which * 8 + 8, part * 128 : (part + 1) * 128],
                out_sem.at[which, part],
            )
            for part in range(3)
        ]

    @pl.loop(0, 8)
    def _(pair):
        for band in range(KG):
            for seg in range(NSEG):
                for which in range(2):
                    v = white_ref[band, 2 * pair + which, seg : seg + 1, :]
                    u = sign * pltpu.roll(v, half, 1)
                    lanes = slice(which * 128, which * 128 + 128)
                    weight_v[band % 2, seg * 128 : seg * 128 + half, lanes] = jnp.where(same, v, 0.0).astype(BF16)
                    weight_v[band % 2, seg * 128 + half : seg * 128 + 128, lanes] = jnp.where(same, u, 0.0).astype(BF16)
            cross = dot(all_v[:, band * 1024 : (band + 1) * 1024], weight_v[band % 2]).astype(BF16)
            for which in range(2):
                cross_v[which, :, band * 128 : (band + 1) * 128] = cross[:, which * 128 : (which + 1) * 128]
        for which in range(2):
            lags = dot(cross_v[which], lag_ref[...])
            spot = lax.rem(pair, 4) * 2 + which
            for part in range(3):
                out_v[pair // 4, part, pl.ds(spot, SRC, stride=8), :] = lags[:, part * 128 : (part + 1) * 128]
        for which in range(2):

            @pl.when(pair == which * 4 + 3)
            def _():
                for copy in copies(which):
                    copy.start()

    for which in range(2):
        for copy in copies(which):
            copy.wait()


def local(raw_strain, fir_taps, source_channels, live_counts):
    rev = jnp.pad(jnp.flip(fir_taps), (1, 384 - 1 - TAPS))[None, :]
    src = source_channels[None, :]
    any_spec = pl.BlockSpec(memory_space=pl.ANY)
    vmem = pl.BlockSpec(memory_space=pltpu.VMEM)
    dma = pltpu.SemaphoreType.DMA
    widths = [bands * 128 for _, bands in PARTS]
    hops = NX - 1 + NY - 1 + NZ - 1
    blocks = NX + NY + NZ
    a, b, c, white = pl.pallas_call(
        gather_kernel,
        out_shape=(
            jax.ShapeDtypeStruct((NC, NZ, NY, NX, 16, widths[0]), BF16),
            jax.ShapeDtypeStruct((NC, NX, NZ, NY, 16, widths[1]), BF16),
            jax.ShapeDtypeStruct((NC, NY, NX, NZ, 16, widths[2]), BF16),
            jax.ShapeDtypeStruct((KG, 16 * NSEG, 128), F32),
        ),
        in_specs=[any_spec, vmem, vmem, pl.BlockSpec(memory_space=pltpu.SMEM), any_spec],
        out_specs=(vmem, vmem, vmem, vmem),
        scratch_shapes=[
            pltpu.VMEM((256, 5248), BF16),
            pltpu.VMEM((256, REACH), BF16),
            pltpu.VMEM((256, HALF), BF16),
            pltpu.VMEM((2, 16, HALF), BF16),
            pltpu.VMEM((16, HALF), BF16),
            pltpu.VMEM((TM, 16, HALF), BF16),
            pltpu.VMEM((HALF, 2 * SEG), BF16),
            pltpu.VMEM((16, SEG), BF16),
            dma((4,)),
            dma,
            dma((2,)),
            dma((2,)),
            dma((TM - 1,)),
            dma((TM - 1,)),
            dma((hops,)),
            dma((hops,)),
            dma((hops,)),
            dma((hops,)),
            dma((hops,)),
            dma((hops,)),
            dma((3,)),
            dma((blocks,)),
            dma((blocks,)),
        ],
        compiler_params=pltpu.CompilerParams(
            collective_id=0, has_side_effects=True, vmem_limit_bytes=60 * 1024 * 1024
        ),
        name="filter_and_gather",
    )(raw_strain, rev, src, live_counts, jnp.asarray(dft_table()))
    return pl.pallas_call(
        correlate_kernel,
        out_shape=jax.ShapeDtypeStruct((SRC, 16, 2 * LAGH), F32),
        in_specs=[vmem, vmem, vmem, vmem, vmem, vmem],
        out_specs=any_spec,
        scratch_shapes=[
            pltpu.VMEM((SRC, NSEG * SEG), BF16),
            pltpu.VMEM((2, SEG, 256), BF16),
            pltpu.VMEM((2, SRC, SEG), BF16),
            pltpu.VMEM((2, 3, SRC * 8, 128), F32),
            dma((2, 3)),
        ],
        compiler_params=pltpu.CompilerParams(vmem_limit_bytes=60 * 1024 * 1024),
        name="correlate",
    )(src, white.reshape(KG, 16, NSEG, 128), a, b, c, jnp.asarray(lag_table()))


def solution(mesh):
    placed = (P("chan", "tm"), P(), P(), P(("chan", "tm")))
    return jax.shard_map(
        local, mesh=mesh, in_specs=placed, out_specs=P(None, ("chan", "tm"), None), check_vma=False
    )
```

```python
import functools
import math

import jax
import jax.numpy as jnp
import numpy as np
from jax import lax
from jax.experimental import pallas as pl
from jax.experimental.pallas import tpu as pltpu
from jax.sharding import PartitionSpec as P

NX, NY, NZ, NC = 4, 4, 8, 2
TM, CHAN = 16, 16
DECIM, SEG, BAND, LAGH = 10, 1024, 64, 192
NSEG = 8
HALF = SEG // 2
SRC = 256
SLOTS = 512
EPS = 1e-06
MESH = pl.DeviceIdType.MESH
F32, BF16 = jnp.float32, jnp.bfloat16
TAPS = 128
REACH = 1408
KG = HALF // BAND
QUARTERS, BINS = 4, 16
QUOTA = SRC // NX
PARTS = ((0, 16), (16, 16), (32, 32))
ROUNDS = "ABCABACABABCAC"


def dot(a, b):
    return jnp.dot(a, b, preferred_element_type=F32)


def hi_lo(table):
    hi = table.astype(np.float32).astype(jnp.bfloat16)
    lo = (table - hi.astype(np.float64)).astype(np.float32).astype(jnp.bfloat16)
    return hi, lo


def dft_table():
    n = np.arange(HALF)[:, None]
    k = np.arange(HALF)[None, :]
    phase = (n * k % SEG) * (2.0 * np.pi / SEG)
    both = np.stack([np.cos(phase), -np.sin(phase)], axis=1).reshape(HALF, 2, KG, QUARTERS, BINS)
    table = both.transpose(0, 2, 3, 1, 4).reshape(HALF, SEG)
    return np.concatenate(hi_lo(table), axis=1)


def lag_table():
    k = np.arange(HALF)[:, None]
    t = np.arange(-LAGH, LAGH)[None, :]
    phase = (k * t % SEG) * (2.0 * np.pi / SEG)
    weight = np.where(k == 0, 1.0, 2.0) * (math.sqrt(SEG / NSEG) / SEG)
    both = np.stack([weight * np.cos(phase), -weight * np.sin(phase)], axis=0)
    table = both.reshape(2, KG, QUARTERS, BINS, 2 * LAGH).transpose(1, 2, 0, 3, 4).reshape(SEG, 2 * LAGH)
    return table.astype(np.float32).astype(jnp.bfloat16)


def whiten(spec, turn=None):
    bands = []
    for band in range(KG):
        block = spec[:, band * 128 : (band + 1) * 128]
        power = jnp.sum(block * block, axis=1, keepdims=True) * (1.0 / BAND)
        block = block * lax.rsqrt(power + EPS)
        bands.append(block if turn is None else pltpu.roll(block, turn, 1))
    return jnp.concatenate(bands, axis=1).astype(BF16)


def odd_sign(rows):
    lane = lax.broadcasted_iota(jnp.int32, (rows, SEG), 1)
    return (1 - 2 * lax.rem(lane, 2)).astype(F32)


def place(x, y, z, core):
    return (y * 4 + z // 2, lax.rem(z, 2) * 8 + x * 2 + core)


def gather_part(semaphores, order, step_dir, sends, first):
    send_sem, recv_sem = semaphores
    count = 0
    for stage, (me, size, chunk, device) in enumerate(order):

        def index(offset):
            return lax.rem(me + step_dir * offset + size, size)

        def copy_of(src, to, number):
            return pltpu.make_async_remote_copy(
                src_ref=src[0],
                dst_ref=src[1],
                send_sem=send_sem.at[number],
                recv_sem=recv_sem.at[number],
                device_id=device(index(to)),
                device_id_type=MESH,
            )

        def send(src, dst, to, number):
            copy = copy_of((src, dst), to, number)
            copy.start()
            sends.append(copy)

        def arrived(offset, number):
            block = chunk(index(offset))
            copy_of((block, block), 1, number).wait_recv()
            return block

        own = chunk(me)
        start = first if stage == 0 else own
        if stage < len(order) - 1:
            for offset in range(1, size):
                send(start, own, offset, count + offset - 1)
            yield None
            for offset in range(1, size):
                arrived(-offset, count + offset - 1)
            count += size - 1
            continue
        far, near = size // 2, size - 1 - size // 2
        send(own, own, 1, count)
        send(own, own, -1, count + far)
        yield own
        for hop in range(1, far + 1):
            yield None
            block = arrived(-hop, count + hop - 1)
            if hop < far:
                send(block, block, 1, count + hop)
            yield block
            if hop <= near:
                block = arrived(hop, count + far + hop - 1)
                if hop < near:
                    send(block, block, -1, count + far + hop)
                yield block


def gather_kernel(
    raw_hbm, rev_ref, src_ref, live_ref, table_hbm,
    a_ref, b_ref, c_ref, white_ref,
    raw_v, tap_v, dec_v, sel_v, pair_v, trace_v, table_v, own_v, slot_v, place_v, block_v,
    load_sem, table_sem, halo_sem, pair_sem, trace_send, trace_recv,
    a_send, a_recv, b_send, b_recv, c_send, c_recv, own_sem, twin_send, twin_recv, spread_send, spread_recv,
):
    tm = lax.axis_index("tm")
    chan = lax.axis_index("chan")
    y, z_hi = tm // 4, lax.rem(tm, 4)
    z_lo, x, core = chan // 8, lax.rem(chan, 8) // 2, lax.rem(chan, 2)
    z = z_hi * 2 + z_lo
    direction = 1 - 2 * core
    half = lax.rem(tm, 2)

    def remote(src, dst, sems, device):
        return pltpu.make_async_remote_copy(
            src_ref=src, dst_ref=dst, send_sem=sems[0], recv_sem=sems[1], device_id=device, device_id_type=MESH
        )

    loads = []
    for part in range(4):
        loads.append(
            pltpu.make_async_copy(
                raw_hbm.at[:, part * 1280 : (part + 1) * 1280],
                raw_v.at[:, 128 + part * 1280 : 128 + (part + 1) * 1280],
                load_sem.at[part],
            )
        )
        loads[-1].start()
    table_load = pltpu.make_async_copy(table_hbm, table_v, table_sem)
    table_load.start()

    barrier = pltpu.get_barrier_semaphore()
    peers = [(lax.rem(tm + step, TM), chan) for step in range(1, TM)]
    twin = place(x, y, z, 1 - core)
    run = lax.rem(z, 4)
    spread = []
    for step in range(1, 32):
        to_run = lax.rem(run + step // 8, 4)
        to_x = lax.rem(x + step // 2, NX)
        to_core = lax.rem(core + step, NC)
        spread.append((place(to_x, y, z - run + to_run, to_core), to_run * 2 + to_core))
        peers.append(spread[-1][0])
    for step in (1, 3, 5, 7):
        peers.append(place(x, y, lax.rem(z + step, NZ), core))
    for peer in peers:
        pl.semaphore_signal(barrier, inc=1, device_id=peer, device_id_type=MESH)
    pl.semaphore_wait(barrier, len(peers))

    halo = remote(
        raw_hbm.at[:, 4992:5120], raw_v.at[:, 0:128], (halo_sem.at[0], halo_sem.at[1]), (lax.rem(tm + 1, TM), chan)
    )
    halo.start()

    base = pltpu.roll(jnp.broadcast_to(rev_ref[...], (8, 384)), 0, 1, stride=DECIM, stride_axis=0)
    for group in range(8):
        rows = []
        for octet in (2 * group, 2 * group + 1):
            at, turn = divmod(octet * 8 * DECIM, 128)
            piece = pltpu.roll(base, turn, 1) if turn else base
            blocks = [jnp.zeros((8, 128), F32)] * (REACH // 128)
            for number in range(min(3, REACH // 128 - at)):
                blocks[at + number] = piece[:, number * 128 : (number + 1) * 128]
            rows.append(jnp.concatenate(blocks, axis=1))
        band = jnp.concatenate(rows, axis=0)
        band_hi = band.astype(BF16)
        tap_v[group * 16 : group * 16 + 16, :] = band_hi
        tap_v[128 + group * 16 : 128 + group * 16 + 16, :] = (band - band_hi.astype(F32)).astype(BF16)

    src = src_ref[...].astype(F32)
    src_col = jnp.transpose(jnp.broadcast_to(src, (SRC, SRC)))
    lane = lax.broadcasted_iota(jnp.int32, (SRC, SRC), 1)
    row = lax.broadcasted_iota(jnp.int32, (SRC, SRC), 0)
    hit = jnp.where(src_col == (lane + chan * 256).astype(F32), 1.0, 0.0)
    is_src = jnp.sum(hit, axis=0, keepdims=True)
    earlier = jnp.where((row // 16 == lane // 16) & (row < lane), 1.0, 0.0)
    rank = dot(jnp.broadcast_to(is_src, (16, SRC)).astype(BF16), earlier.astype(BF16))[0:1, :]
    pick_row = lax.broadcasted_iota(jnp.int32, (32, SRC), 0)
    pick_lane = lax.broadcasted_iota(jnp.int32, (32, SRC), 1)
    pick = jnp.where(
        (pick_row // 2 == pick_lane // 16) & (lax.rem(pick_row, 2).astype(F32) == rank) & (is_src > 0.5), 1.0, 0.0
    ).astype(BF16)

    src_row = jnp.broadcast_to(src, (SRC, SRC))
    row_block = jnp.floor(src_row * (1.0 / 16))
    col_block = jnp.floor(src_col * (1.0 / 16))
    before = jnp.where((row_block == col_block) & (src_row < src_col), 1.0, 0.0)
    behind = jnp.sum(before, axis=1, keepdims=True).astype(jnp.int32)
    block_of = col_block[:, 0:1].astype(jnp.int32)
    chan_of, local_of = block_of // 16, lax.rem(block_of, 16)
    spot = ((local_of // 8) * 2 + chan_of // 8) * 128 + lax.rem(chan_of, 8) * 16 + 2 * lax.rem(local_of, 8) + behind
    place_v[...] = jnp.broadcast_to(spot, (SRC, 128))

    for part in (1, 2, 3, 0):
        if part == 1:
            loads[0].wait()
        if part:
            loads[part].wait()
        else:
            halo.wait()

            @pl.when(tm == 0)
            def _():
                raw_v[:, 0:128] = jnp.zeros((256, 128), BF16)

        both = lax.dot_general(
            raw_v[:, part * 1280 : part * 1280 + REACH],
            tap_v[...],
            (((1,), (1,)), ((), ())),
            preferred_element_type=F32,
        )
        dec_v[:, part * 128 : (part + 1) * 128] = (both[:, 0:128] + both[:, 128:256]).astype(BF16)

    picked = dot(pick, dec_v[...]).astype(BF16)
    sel_v[0] = picked[0:16]
    sel_v[1] = picked[16:32]
    pair = remote(
        sel_v.at[1 - half], pair_v, (pair_sem.at[0], pair_sem.at[1]), (tm + 1 - 2 * half, chan)
    )
    pair.start()

    pair.wait()
    traces = []
    for step in range(1, TM):
        to = lax.rem(tm + step, TM)
        copy = remote(
            dec_v.at[pl.ds(pl.multiple_of(to * 16, 16), 16), :],
            trace_v.at[tm],
            (trace_send.at[step - 1], trace_recv.at[step - 1]),
            (to, chan),
        )
        copy.start()
        traces.append(copy)
    trace_v[tm] = dec_v[pl.ds(pl.multiple_of(tm * 16, 16), 16), :]

    table_load.wait()
    spec = dot(jnp.concatenate([sel_v[half], pair_v[...]], axis=0), table_v[...])
    mine = spec[0:16, 0:SEG] + spec[0:16, SEG:]
    other = spec[16:32, 0:SEG] + spec[16:32, SEG:]
    is_first = half == 0
    sign = odd_sign(16)
    full = whiten(
        jnp.where(is_first, mine, other) + sign * jnp.where(is_first, other, mine), 32 * lax.rem(tm // 2, 4)
    )
    for band in range(KG):
        own_v[band] = full[:, band * 128 : (band + 1) * 128]

    here = run * 8 + x * 2 + core
    spreads = []
    for number, (peer, band) in enumerate(spread):
        copy = remote(own_v.at[band], slot_v.at[here], (spread_send.at[number], spread_recv.at[number]), peer)
        copy.start()
        spreads.append(copy)
    slot_v[here] = own_v[run * 2 + core]
    wanted = place_v[pl.ds(pl.multiple_of(x * QUOTA, QUOTA), QUOTA), :]
    slot_lane = lax.broadcasted_iota(jnp.int32, (QUOTA, 128), 1)
    chosen = jnp.concatenate(
        [jnp.where(wanted == slot_lane + part * 128, 1.0, 0.0) for part in range(SLOTS // 128)], axis=1
    ).astype(BF16)
    for copy in spreads:
        copy.wait()
    block_v[...] = dot(chosen, slot_v[...].reshape(SLOTS, 128)).astype(BF16)

    def part_order(buf, axes):
        sizes = {"x": NX, "y": NY, "z": NZ}
        at = {"x": x, "y": y, "z": z}
        order = []
        for number, axis in enumerate(axes):
            lead = [at[a] for a in reversed(axes[number + 1 :])]

            def chunk(index, lead=lead):
                return buf.at[(core, *lead, index)]

            def device(index, axis=axis):
                where = dict(at)
                where[axis] = index
                return place(where["x"], where["y"], where["z"], core)

            order.append((at[axis], sizes[axis], chunk, device))
        return order

    sends = []
    routines = []
    own_copies = []
    bufs = ((a_ref, "xyz", a_send, a_recv), (b_ref, "yzx", b_send, b_recv), (c_ref, "zxy", c_send, c_recv))
    for number, (buf, axes, send_sem, recv_sem) in enumerate(bufs):
        begin, rows = PARTS[number]
        first = block_v.at[begin : begin + rows]
        at = {"x": x, "y": y, "z": z}
        slot = buf.at[(core, *(at[a] for a in reversed(axes)))]
        copy = pltpu.make_async_copy(first, slot, own_sem.at[number])
        copy.start()
        own_copies.append(copy)
        order = part_order(buf, axes)
        routines.append(gather_part((send_sem, recv_sem), order, direction, sends, first))

    twins = []

    def to_twin(block):
        number = len(twins)
        copy = remote(block, block, (twin_send.at[number], twin_recv.at[number]), twin)
        copy.start()
        twins.append(copy)

    def advance(name):
        for block in routines["ABC".index(name)]:
            if block is None:
                break
            to_twin(block)

    def own_channels(part):
        rows = lax.broadcasted_iota(jnp.int32, (128, HALF), 0)
        alive = lax.rem(rows, 16) < live_ref[0]
        flat = trace_v[part * 8 : part * 8 + 8].reshape(128, HALF)
        spec = dot(jnp.where(alive, flat, jnp.zeros_like(flat)), table_v[...])
        for seg in range(NSEG // 2):
            low = spec[seg * 32 : seg * 32 + 16]
            high = spec[seg * 32 + 16 : seg * 32 + 32]
            full = low[:, 0:SEG] + low[:, SEG:] + sign * (high[:, 0:SEG] + high[:, SEG:])
            white = whiten(full).astype(F32)
            for band in range(KG):
                rows_at = pl.ds(part * 4 + seg, 16, stride=NSEG)
                white_ref[band, rows_at, :] = white[:, band * 128 : (band + 1) * 128]

    for name in "ABC":
        advance(name)
    for copy in own_copies:
        copy.wait()
    for copy in traces:
        copy.wait()
    own_channels(0)
    for number, name in enumerate(ROUNDS):
        if number == 4:
            own_channels(1)
        advance(name)
    for copy in sends:
        copy.wait_send()
    for copy in twins:
        copy.wait()


def correlate_kernel(white_ref, a_ref, b_ref, c_ref, lag_ref, out_hbm, all_v, weight_v, cross_v, out_v, out_sem):
    quarter = lax.broadcasted_iota(jnp.int32, (SRC, 128), 1) // 32
    quarter_b = quarter.astype(F32).astype(BF16)

    def merge(blocks, shift):
        full = blocks[(0 - shift) % 4]
        lanes = (quarter_b if full.dtype == BF16 else quarter)[0 : full.shape[0]]
        for j in range(1, 4):
            full = jnp.where(lanes == j, blocks[(j - shift) % 4], full)
        return full

    for band in range(KG):
        run, core = band // 2, band % 2
        for four in range(2):
            blocks = []
            for seg in range(four * 4, four * 4 + 4):
                y, z = seg // 2, (seg % 2) * 4 + run
                pieces = []
                for x in range(NX):
                    pieces += [a_ref[core, z, y, x], b_ref[core, x, z, y], c_ref[core, y, x, z]]
                blocks.append(jnp.concatenate(pieces, axis=0))
            for part in range(QUARTERS):
                lane = ((band * QUARTERS + part) * 2 + four) * 128
                all_v[:, lane : lane + 128] = merge(blocks, part)

    row = lax.broadcasted_iota(jnp.int32, (BINS, 128), 0)
    lane = lax.broadcasted_iota(jnp.int32, (BINS, 128), 1)
    same = row.astype(F32).astype(BF16) == lax.rem(lane, BINS).astype(F32).astype(BF16)

    def spread(rows, seg):
        wide = jnp.broadcast_to(rows[seg : seg + 1], (BINS, 128)).astype(BF16)
        return jnp.where(same, wide, jnp.zeros_like(wide))

    is_re = lax.rem(lane[0:8], 2 * BINS) < BINS

    def copies(which):
        return [
            pltpu.make_async_copy(
                out_v.at[which, part].reshape(SRC, 8, 128),
                out_hbm.at[:, which * 8 : which * 8 + 8, part * 128 : (part + 1) * 128],
                out_sem.at[which, part],
            )
            for part in range(3)
        ]

    @pl.loop(0, 2)
    def _(octet):
        @pl.loop(0, 4)
        def _(band_pair):
          for sub in range(2):
            band = band_pair * 2 + sub
            crosses = []
            turned = [pltpu.roll(white_ref[band, 8 * octet + c], 32 * (c % 4), 1) if c % 4 else white_ref[band, 8 * octet + c] for c in range(8)]
            for part in range(QUARTERS):
                slot = part % 2
                for group in range(2):
                    v = merge(turned[group * 4 : group * 4 + 4], part)
                    u = jnp.where(is_re, pltpu.roll(v, 128 - BINS, 1), -pltpu.roll(v, BINS, 1))
                    lanes = slice(group * 128, group * 128 + 128)
                    for four in range(2):
                        for j in range(4):
                            seg = four * 4 + (j - part) % 4
                            at = four * 128 + j * 32
                            weight_v[slot, at : at + 16, lanes] = spread(v, seg)
                            weight_v[slot, at + 16 : at + 32, lanes] = spread(u, seg)
                at = pl.multiple_of((band * QUARTERS + part) * 256, 256)
                crosses.append(dot(all_v[:, pl.ds(at, 256)], weight_v[slot]).astype(BF16))
            for c in range(8):
                blocks = [cross[:, c // 4 * 128 : c // 4 * 128 + 128] for cross in crosses]
                full = blocks[0]
                for part in range(1, 4):
                    full = jnp.where(quarter_b == (c + part) % 4, blocks[part], full)
                cross_v[c, :, pl.ds(pl.multiple_of(band * 128, 128), 128)] = full
        @pl.loop(0, 2)
        def _(four):
            for c in range(4):
                table = jnp.concatenate(
                    [
                        lag_ref[band * 128 + (j - c) % 4 * 32 : band * 128 + (j - c) % 4 * 32 + 32, :]
                        for band in range(KG)
                        for j in range(4)
                    ],
                    axis=0,
                )
                lags = dot(cross_v[four * 4 + c], table)
                for part in range(3):
                    out_v[octet, part, pl.ds(four * 4 + c, SRC, stride=8), :] = lags[:, part * 128 : (part + 1) * 128]

        for which in range(2):

            @pl.when(octet == which)
            def _():
                for copy in copies(which):
                    copy.start()

    for which in range(2):
        for copy in copies(which):
            copy.wait()


def local(raw_strain, fir_taps, source_channels, live_counts):
    rev = jnp.pad(jnp.flip(fir_taps), (1, 384 - 1 - TAPS))[None, :]
    src = source_channels[None, :]
    any_spec = pl.BlockSpec(memory_space=pl.ANY)
    vmem = pl.BlockSpec(memory_space=pltpu.VMEM)
    dma = pltpu.SemaphoreType.DMA
    heights = [rows for _, rows in PARTS]
    hops = NX - 1 + NY - 1 + NZ - 1
    blocks = NX + NY + NZ
    a, b, c, white = pl.pallas_call(
        gather_kernel,
        out_shape=(
            jax.ShapeDtypeStruct((NC, NZ, NY, NX, heights[0], 128), BF16),
            jax.ShapeDtypeStruct((NC, NX, NZ, NY, heights[1], 128), BF16),
            jax.ShapeDtypeStruct((NC, NY, NX, NZ, heights[2], 128), BF16),
            jax.ShapeDtypeStruct((KG, 16 * NSEG, 128), F32),
        ),
        in_specs=[any_spec, vmem, vmem, pl.BlockSpec(memory_space=pltpu.SMEM), any_spec],
        out_specs=(vmem, vmem, vmem, vmem),
        scratch_shapes=[
            pltpu.VMEM((256, 5248), BF16),
            pltpu.VMEM((256, REACH), BF16),
            pltpu.VMEM((256, HALF), BF16),
            pltpu.VMEM((2, 16, HALF), BF16),
            pltpu.VMEM((16, HALF), BF16),
            pltpu.VMEM((TM, 16, HALF), BF16),
            pltpu.VMEM((HALF, 2 * SEG), BF16),
            pltpu.VMEM((KG, 16, 128), BF16),
            pltpu.VMEM((32, 16, 128), BF16),
            pltpu.VMEM((SRC, 128), jnp.int32),
            pltpu.VMEM((QUOTA, 128), BF16),
            dma((4,)),
            dma,
            dma((2,)),
            dma((2,)),
            dma((TM - 1,)),
            dma((TM - 1,)),
            dma((hops,)),
            dma((hops,)),
            dma((hops,)),
            dma((hops,)),
            dma((hops,)),
            dma((hops,)),
            dma((3,)),
            dma((blocks,)),
            dma((blocks,)),
            dma((31,)),
            dma((31,)),
        ],
        compiler_params=pltpu.CompilerParams(
            collective_id=0, has_side_effects=True, vmem_limit_bytes=60 * 1024 * 1024
        ),
        name="filter_and_gather",
    )(raw_strain, rev, src, live_counts, jnp.asarray(dft_table()))
    return pl.pallas_call(
        correlate_kernel,
        out_shape=jax.ShapeDtypeStruct((SRC, 16, 2 * LAGH), F32),
        in_specs=[vmem, vmem, vmem, vmem, vmem],
        out_specs=any_spec,
        scratch_shapes=[
            pltpu.VMEM((SRC, NSEG * SEG), BF16),
            pltpu.VMEM((2, 256, 256), BF16),
            pltpu.VMEM((8, SRC, SEG), BF16),
            pltpu.VMEM((2, 3, SRC * 8, 128), F32),
            dma((2, 3)),
        ],
        compiler_params=pltpu.CompilerParams(vmem_limit_bytes=60 * 1024 * 1024),
        name="correlate",
    )(white.reshape(KG, 16, NSEG, 128), a, b, c, jnp.asarray(lag_table()))


def solution(mesh):
    placed = (P("chan", "tm"), P(), P(), P(("chan", "tm")))
    return jax.shard_map(
        local, mesh=mesh, in_specs=placed, out_specs=P(None, ("chan", "tm"), None), check_vma=False
    )
```

```python
import functools
import math

import jax
import jax.numpy as jnp
import numpy as np
from jax import lax
from jax.experimental import pallas as pl
from jax.experimental.pallas import tpu as pltpu
from jax.sharding import PartitionSpec as P

NX, NY, NZ, NC = 4, 4, 8, 2
TM, CHAN = 16, 16
DECIM, SEG, BAND, LAGH = 10, 1024, 64, 192
NSEG = 8
HALF = SEG // 2
SRC = 256
SLOTS = 512
EPS = 1e-06
MESH = pl.DeviceIdType.MESH
F32, BF16 = jnp.float32, jnp.bfloat16
TAPS = 128
REACH = 1408
KG = HALF // BAND
EDGE = 16
QUARTERS, BINS = 4, 16
QUOTA = SRC // NX
PARTS = ((0, 16), (16, 16), (32, 32))
ROUNDS = "ABCABACABABCAC"


def dot(a, b):
    return jnp.dot(a, b, preferred_element_type=F32)


def hi_lo(table):
    hi = table.astype(np.float32).astype(jnp.bfloat16)
    lo = (table - hi.astype(np.float64)).astype(np.float32).astype(jnp.bfloat16)
    return hi, lo


def dft_table():
    n = np.arange(HALF)[:, None]
    k = np.arange(HALF)[None, :]
    phase = (n * k % SEG) * (2.0 * np.pi / SEG)
    both = np.stack([np.cos(phase), -np.sin(phase)], axis=1).reshape(HALF, 2, KG, QUARTERS, BINS)
    table = both.transpose(0, 2, 3, 1, 4).reshape(HALF, SEG)
    return np.concatenate(hi_lo(table), axis=1)


def lag_table():
    k = np.arange(HALF)[:, None]
    t = np.arange(-LAGH, LAGH)[None, :]
    phase = (k * t % SEG) * (2.0 * np.pi / SEG)
    weight = np.where(k == 0, 1.0, 2.0) * (math.sqrt(SEG / NSEG) / SEG)
    both = np.stack([weight * np.cos(phase), -weight * np.sin(phase)], axis=0)
    table = both.reshape(2, KG, QUARTERS, BINS, 2 * LAGH).transpose(1, 2, 0, 3, 4).reshape(SEG, 2 * LAGH)
    return table.astype(np.float32).astype(jnp.bfloat16)


def whiten(spec, turn=None):
    bands = []
    for band in range(KG):
        block = spec[:, band * 128 : (band + 1) * 128]
        power = jnp.sum(block * block, axis=1, keepdims=True) * (1.0 / BAND)
        block = block * lax.rsqrt(power + EPS)
        bands.append(block if turn is None else pltpu.roll(block, turn, 1))
    return jnp.concatenate(bands, axis=1).astype(BF16)


def odd_sign(rows):
    lane = lax.broadcasted_iota(jnp.int32, (rows, SEG), 1)
    return (1 - 2 * lax.rem(lane, 2)).astype(F32)


def place(x, y, z, core):
    return (y * 4 + z // 2, lax.rem(z, 2) * 8 + x * 2 + core)


def gather_part(semaphores, order, step_dir, sends, first):
    send_sem, recv_sem = semaphores
    count = 0
    for stage, (me, size, chunk, device) in enumerate(order):

        def index(offset):
            return lax.rem(me + step_dir * offset + size, size)

        def copy_of(src, to, number):
            return pltpu.make_async_remote_copy(
                src_ref=src[0],
                dst_ref=src[1],
                send_sem=send_sem.at[number],
                recv_sem=recv_sem.at[number],
                device_id=device(index(to)),
                device_id_type=MESH,
            )

        def send(src, dst, to, number):
            copy = copy_of((src, dst), to, number)
            copy.start()
            sends.append(copy)

        def arrived(offset, number):
            block = chunk(index(offset))
            copy_of((block, block), 1, number).wait_recv()
            return block

        own = chunk(me)
        start = first if stage == 0 else own
        if stage < len(order) - 1:
            for offset in range(1, size):
                send(start, own, offset, count + offset - 1)
            yield None
            for offset in range(1, size):
                arrived(-offset, count + offset - 1)
            count += size - 1
            continue
        far, near = size // 2, size - 1 - size // 2
        send(own, own, 1, count)
        send(own, own, -1, count + far)
        yield own
        for hop in range(1, far + 1):
            yield None
            block = arrived(-hop, count + hop - 1)
            if hop < far:
                send(block, block, 1, count + hop)
            yield block
            if hop <= near:
                block = arrived(hop, count + far + hop - 1)
                if hop < near:
                    send(block, block, -1, count + far + hop)
                yield block


def gather_kernel(
    raw_hbm, taps_ref, src_ref, live_ref, table_hbm,
    a_ref, b_ref, c_ref, white_ref,
    raw_v, tap_v, dec_v, sel_v, pair_v, edge_v, trace_v, table_v, own_v, slot_v, place_v, block_v,
    load_sem, table_sem, halo_sem, pair_sem, trace_send, trace_recv,
    a_send, a_recv, b_send, b_recv, c_send, c_recv, own_sem, twin_send, twin_recv, spread_send, spread_recv,
):
    tm = lax.axis_index("tm")
    chan = lax.axis_index("chan")
    y, z_hi = tm // 4, lax.rem(tm, 4)
    z_lo, x, core = chan // 8, lax.rem(chan, 8) // 2, lax.rem(chan, 2)
    z = z_hi * 2 + z_lo
    direction = 1 - 2 * core
    half = lax.rem(tm, 2)

    def remote(src, dst, sems, device):
        return pltpu.make_async_remote_copy(
            src_ref=src, dst_ref=dst, send_sem=sems[0], recv_sem=sems[1], device_id=device, device_id_type=MESH
        )

    loads = []
    for part in range(4):
        loads.append(
            pltpu.make_async_copy(
                raw_hbm.at[:, part * 1280 : (part + 1) * 1280],
                raw_v.at[:, 128 + part * 1280 : 128 + (part + 1) * 1280],
                load_sem.at[part],
            )
        )
        loads[-1].start()
    table_load = pltpu.make_async_copy(table_hbm, table_v, table_sem)
    table_load.start()

    barrier = pltpu.get_barrier_semaphore()
    peers = [(lax.rem(tm + step, TM), chan) for step in range(1, TM)]
    twin = place(x, y, z, 1 - core)
    run = lax.rem(z, 4)
    spread = []
    for step in range(1, 32):
        to_run = lax.rem(run + step // 8, 4)
        to_x = lax.rem(x + step // 2, NX)
        to_core = lax.rem(core + step, NC)
        spread.append((place(to_x, y, z - run + to_run, to_core), to_run * 2 + to_core))
        peers.append(spread[-1][0])
    for step in (1, 3, 5, 7):
        peers.append(place(x, y, lax.rem(z + step, NZ), core))
    for peer in peers:
        pl.semaphore_signal(barrier, inc=1, device_id=peer, device_id_type=MESH)
    taps_col = jnp.transpose(jnp.broadcast_to(taps_ref[...], (TAPS, TAPS)))
    tap_row = lax.broadcasted_iota(jnp.int32, (TAPS, 384), 0)
    tap_lane = lax.broadcasted_iota(jnp.int32, (TAPS, 384), 1)
    taps_wide = jnp.concatenate([taps_col] * 3, axis=1)
    rev = jnp.sum(jnp.where(tap_row + tap_lane == TAPS, taps_wide, 0.0), axis=0, keepdims=True)
    base = pltpu.roll(jnp.broadcast_to(rev, (8, 384)), 0, 1, stride=DECIM, stride_axis=0)
    for group in range(8):
        rows = []
        for octet in (2 * group, 2 * group + 1):
            at, turn = divmod(octet * 8 * DECIM, 128)
            piece = pltpu.roll(base, turn, 1) if turn else base
            blocks = [jnp.zeros((8, 128), F32)] * (REACH // 128)
            for number in range(min(3, REACH // 128 - at)):
                blocks[at + number] = piece[:, number * 128 : (number + 1) * 128]
            rows.append(jnp.concatenate(blocks, axis=1))
        band = jnp.concatenate(rows, axis=0)
        band_hi = band.astype(BF16)
        tap_v[group * 16 : group * 16 + 16, :] = band_hi
        tap_v[128 + group * 16 : 128 + group * 16 + 16, :] = (band - band_hi.astype(F32)).astype(BF16)

    src = src_ref[...].astype(F32)
    src_col = jnp.transpose(jnp.broadcast_to(src, (SRC, SRC)))
    lane = lax.broadcasted_iota(jnp.int32, (SRC, SRC), 1)
    row = lax.broadcasted_iota(jnp.int32, (SRC, SRC), 0)
    hit = jnp.where(src_col == (lane + chan * 256).astype(F32), 1.0, 0.0)
    is_src = jnp.sum(hit, axis=0, keepdims=True)
    earlier = jnp.where((row // 16 == lane // 16) & (row < lane), 1.0, 0.0)
    rank = dot(jnp.broadcast_to(is_src, (16, SRC)).astype(BF16), earlier.astype(BF16))[0:1, :]
    pick_row = lax.broadcasted_iota(jnp.int32, (32, SRC), 0)
    pick_lane = lax.broadcasted_iota(jnp.int32, (32, SRC), 1)
    pick = jnp.where(
        (pick_row // 2 == pick_lane // 16) & (lax.rem(pick_row, 2).astype(F32) == rank) & (is_src > 0.5), 1.0, 0.0
    ).astype(BF16)

    src_row = jnp.broadcast_to(src, (SRC, SRC))
    row_block = jnp.floor(src_row * (1.0 / 16))
    col_block = jnp.floor(src_col * (1.0 / 16))
    before = jnp.where((row_block == col_block) & (src_row < src_col), 1.0, 0.0)
    behind = jnp.sum(before, axis=1, keepdims=True).astype(jnp.int32)
    block_of = col_block[:, 0:1].astype(jnp.int32)
    chan_of, local_of = block_of // 16, lax.rem(block_of, 16)
    spot = ((local_of // 8) * 2 + chan_of // 8) * 128 + lax.rem(chan_of, 8) * 16 + 2 * lax.rem(local_of, 8) + behind
    place_v[...] = jnp.broadcast_to(spot, (SRC, 128))

    def filtered(samples, taps):
        both = lax.dot_general(samples, taps, (((1,), (1,)), ((), ())), preferred_element_type=F32)
        return both[:, 0:128] + both[:, 128:256]

    raw_v[:, 0:128] = jnp.zeros((256, 128), BF16)
    heads = None
    for part in range(4):
        loads[part].wait()
        sums = filtered(raw_v[:, part * 1280 : part * 1280 + REACH], tap_v[...])
        dec_v[:, part * 128 : (part + 1) * 128] = sums.astype(BF16)
        heads = sums if part == 0 else heads
    tails = filtered(raw_v[:, 5120:5248], tap_v[:, 0:128])
    edge_lane = lax.broadcasted_iota(jnp.int32, (256, 128), 1)
    edge = jnp.where(edge_lane < 64, heads, pltpu.roll(tails, 64, 1))
    edge = jnp.where(lax.rem(edge_lane, 64) < EDGE, edge, 0.0)
    packed = jnp.zeros((256, 128), F32)
    for number in range(3):
        piece = edge.astype(BF16).astype(F32)
        edge = edge - piece
        packed = packed + (pltpu.roll(piece, number * EDGE, 1) if number else piece)
    dec_v[:, HALF:] = packed.astype(BF16)

    def joined(main, edges, before):
        def whole(rows, at):
            full = pltpu.roll(rows, 128 - at, 1) if at else rows
            for number in (1, 2):
                full = full + pltpu.roll(rows, 128 - at - number * EDGE, 1)
            return full

        sums = (whole(edges.astype(F32), 0) + whole(before.astype(F32), 64)).astype(BF16)
        lanes = lax.broadcasted_iota(jnp.int32, sums.shape, 1)
        first = jnp.where(lanes < EDGE, sums.astype(F32), main[:, 0:128].astype(F32)).astype(BF16)
        return jnp.concatenate([first, main[:, 128:]], axis=1)

    picked = dot(pick, dec_v[...]).astype(BF16)
    sel_v[0] = picked[0:16]
    sel_v[1] = picked[16:32]
    pl.semaphore_wait(barrier, len(peers))
    pair = remote(sel_v.at[1 - half], pair_v, (pair_sem.at[0], pair_sem.at[1]), (tm + 1 - 2 * half, chan))
    pair.start()
    edge_copies = []
    for step in (1, 2):
        copy = remote(
            sel_v.at[(1 - half) if step == 1 else half, :, HALF:],
            edge_v.at[step - 1],
            (halo_sem.at[0, step - 1], halo_sem.at[1, step - 1]),
            (lax.rem(tm + step, TM), chan),
        )
        copy.start()
        edge_copies.append(copy)

    pair.wait()
    for copy in edge_copies:
        copy.wait()
    traces = []
    for step in range(1, TM):
        to = lax.rem(tm + step, TM)
        copy = remote(
            dec_v.at[pl.ds(pl.multiple_of(to * 16, 16), 16), :],
            trace_v.at[tm],
            (trace_send.at[step - 1], trace_recv.at[step - 1]),
            (to, chan),
        )
        copy.start()
        traces.append(copy)
    trace_v[tm] = dec_v[pl.ds(pl.multiple_of(tm * 16, 16), 16), :]

    table_load.wait()
    is_first = half == 0
    mine, other = sel_v[half].astype(F32), pair_v[...].astype(F32)
    low, high = jnp.where(is_first, mine, other), jnp.where(is_first, other, mine)
    tail = jnp.where(is_first, edge_v[0].astype(F32), edge_v[1].astype(F32))
    tail = jnp.where(tm // 2 == 0, 0.0, tail)
    low_edge, high_edge = low[:, HALF:], high[:, HALF:]
    low = joined(low[:, 0:HALF].astype(BF16), low_edge, tail)
    high = joined(high[:, 0:HALF].astype(BF16), high_edge, low_edge)
    spec = dot(jnp.concatenate([low, high], axis=0), table_v[...])
    sign = odd_sign(16)
    full = whiten(
        spec[0:16, 0:SEG] + spec[0:16, SEG:] + sign * (spec[16:32, 0:SEG] + spec[16:32, SEG:]),
        32 * lax.rem(tm // 2, 4),
    )
    for band in range(KG):
        own_v[band] = full[:, band * 128 : (band + 1) * 128]

    here = run * 8 + x * 2 + core
    spreads = []
    for number, (peer, band) in enumerate(spread):
        copy = remote(own_v.at[band], slot_v.at[here], (spread_send.at[number], spread_recv.at[number]), peer)
        copy.start()
        spreads.append(copy)
    slot_v[here] = own_v[run * 2 + core]
    wanted = place_v[pl.ds(pl.multiple_of(x * QUOTA, QUOTA), QUOTA), :]
    slot_lane = lax.broadcasted_iota(jnp.int32, (QUOTA, 128), 1)
    chosen = jnp.concatenate(
        [jnp.where(wanted == slot_lane + part * 128, 1.0, 0.0) for part in range(SLOTS // 128)], axis=1
    ).astype(BF16)
    for copy in spreads:
        copy.wait()
    block_v[...] = dot(chosen, slot_v[...].reshape(SLOTS, 128)).astype(BF16)

    def part_order(buf, axes):
        sizes = {"x": NX, "y": NY, "z": NZ}
        at = {"x": x, "y": y, "z": z}
        order = []
        for number, axis in enumerate(axes):
            lead = [at[a] for a in reversed(axes[number + 1 :])]

            def chunk(index, lead=lead):
                return buf.at[(core, *lead, index)]

            def device(index, axis=axis):
                where = dict(at)
                where[axis] = index
                return place(where["x"], where["y"], where["z"], core)

            order.append((at[axis], sizes[axis], chunk, device))
        return order

    sends = []
    routines = []
    own_copies = []
    bufs = ((a_ref, "xyz", a_send, a_recv), (b_ref, "yzx", b_send, b_recv), (c_ref, "zxy", c_send, c_recv))
    for number, (buf, axes, send_sem, recv_sem) in enumerate(bufs):
        begin, rows = PARTS[number]
        first = block_v.at[begin : begin + rows]
        at = {"x": x, "y": y, "z": z}
        slot = buf.at[(core, *(at[a] for a in reversed(axes)))]
        copy = pltpu.make_async_copy(first, slot, own_sem.at[number])
        copy.start()
        own_copies.append(copy)
        order = part_order(buf, axes)
        routines.append(gather_part((send_sem, recv_sem), order, direction, sends, first))

    twins = []

    def to_twin(block):
        number = len(twins)
        copy = remote(block, block, (twin_send.at[number], twin_recv.at[number]), twin)
        copy.start()
        twins.append(copy)

    def advance(name):
        for block in routines["ABC".index(name)]:
            if block is None:
                break
            to_twin(block)

    def own_channels(part):
        rows = lax.broadcasted_iota(jnp.int32, (128, HALF), 0)
        alive = lax.rem(rows, 16) < live_ref[0]
        main = trace_v[part * 8 : part * 8 + 8, :, 0:HALF].reshape(128, HALF)
        edges = trace_v[part * 8 : part * 8 + 8, :, HALF:].reshape(128, 128).astype(F32)
        if part:
            before = trace_v[part * 8 - 1, :, HALF:].astype(F32)
        else:
            before = jnp.zeros((16, 128), F32)
        flat = joined(main, edges, jnp.concatenate([before, edges[0:112]], axis=0))
        spec = dot(jnp.where(alive, flat, jnp.zeros_like(flat)), table_v[...])
        for seg in range(NSEG // 2):
            low = spec[seg * 32 : seg * 32 + 16]
            high = spec[seg * 32 + 16 : seg * 32 + 32]
            full = low[:, 0:SEG] + low[:, SEG:] + sign * (high[:, 0:SEG] + high[:, SEG:])
            white = whiten(full).astype(F32)
            for band in range(KG):
                rows_at = pl.ds(part * 4 + seg, 16, stride=NSEG)
                white_ref[band, rows_at, :] = white[:, band * 128 : (band + 1) * 128]

    for name in "ABC":
        advance(name)
    for copy in own_copies:
        copy.wait()
    for copy in traces:
        copy.wait()
    own_channels(0)
    for number, name in enumerate(ROUNDS):
        if number == 4:
            own_channels(1)
        advance(name)
    for copy in sends:
        copy.wait_send()
    for copy in twins:
        copy.wait()


def correlate_kernel(white_ref, a_ref, b_ref, c_ref, lag_ref, out_hbm, all_v, weight_v, cross_v, out_v, out_sem):
    quarter = lax.broadcasted_iota(jnp.int32, (SRC, 128), 1) // 32
    quarter_b = quarter.astype(F32).astype(BF16)

    def merge(blocks, shift, rows=16):
        lanes = (quarter_b if blocks[0].dtype == BF16 else quarter)[0:rows]
        masks = [lanes == j for j in range(4)]
        pieces = []
        for at in range(0, blocks[0].shape[0], rows):
            full = blocks[(0 - shift) % 4][at : at + rows]
            for j in range(1, 4):
                full = jnp.where(masks[j], blocks[(j - shift) % 4][at : at + rows], full)
            pieces.append(full)
        return jnp.concatenate(pieces, axis=0) if len(pieces) > 1 else pieces[0]

    for band in range(KG):
        run, core = band // 2, band % 2
        for four in range(2):
            blocks = []
            for seg in range(four * 4, four * 4 + 4):
                y, z = seg // 2, (seg % 2) * 4 + run
                pieces = []
                for x in range(NX):
                    pieces += [a_ref[core, z, y, x], b_ref[core, x, z, y], c_ref[core, y, x, z]]
                blocks.append(jnp.concatenate(pieces, axis=0))
            for part in range(QUARTERS):
                lane = ((band * QUARTERS + part) * 2 + four) * 128
                all_v[:, lane : lane + 128] = merge(blocks, part)

    row = lax.broadcasted_iota(jnp.int32, (BINS, 128), 0)
    lane = lax.broadcasted_iota(jnp.int32, (BINS, 128), 1)
    same = row.astype(F32).astype(BF16) == lax.rem(lane, BINS).astype(F32).astype(BF16)

    def spread(rows, seg):
        wide = jnp.broadcast_to(rows[seg : seg + 1], (BINS, 128)).astype(BF16)
        return jnp.where(same, wide, jnp.zeros_like(wide))

    is_re = lax.rem(lane[0:8], 2 * BINS) < BINS

    def copies(which):
        return [
            pltpu.make_async_copy(
                out_v.at[which, part].reshape(SRC, 8, 128),
                out_hbm.at[:, which * 8 : which * 8 + 8, part * 128 : (part + 1) * 128],
                out_sem.at[which, part],
            )
            for part in range(3)
        ]

    @pl.loop(0, 2)
    def _(octet):
        @pl.loop(0, 4)
        def _(band_pair):
          for sub in range(2):
            band = band_pair * 2 + sub
            crosses = []
            turned = [pltpu.roll(white_ref[band, 8 * octet + c], 32 * (c % 4), 1) if c % 4 else white_ref[band, 8 * octet + c] for c in range(8)]
            for part in range(QUARTERS):
                slot = part % 2
                for group in range(2):
                    v = merge(turned[group * 4 : group * 4 + 4], part, 8)
                    u = jnp.where(is_re, pltpu.roll(v, 128 - BINS, 1), -pltpu.roll(v, BINS, 1))
                    lanes = slice(group * 128, group * 128 + 128)
                    for four in range(2):
                        for j in range(4):
                            seg = four * 4 + (j - part) % 4
                            at = four * 128 + j * 32
                            weight_v[slot, at : at + 16, lanes] = spread(v, seg)
                            weight_v[slot, at + 16 : at + 32, lanes] = spread(u, seg)
                at = pl.multiple_of((band * QUARTERS + part) * 256, 256)
                crosses.append(dot(all_v[:, pl.ds(at, 256)], weight_v[slot]).astype(BF16))
            for c in range(8):
                blocks = [cross[:, c // 4 * 128 : c // 4 * 128 + 128] for cross in crosses]
                full = merge(blocks, c)
                cross_v[c, :, pl.ds(pl.multiple_of(band * 128, 128), 128)] = full
        @pl.loop(0, 2)
        def _(four):
            for c in range(4):
                table = jnp.concatenate(
                    [
                        lag_ref[band * 128 + (j - c) % 4 * 32 : band * 128 + (j - c) % 4 * 32 + 32, :]
                        for band in range(KG)
                        for j in range(4)
                    ],
                    axis=0,
                )
                lags = dot(cross_v[four * 4 + c], table)
                for part in range(3):
                    out_v[octet, part, pl.ds(four * 4 + c, SRC, stride=8), :] = lags[:, part * 128 : (part + 1) * 128]

        for which in range(2):

            @pl.when(octet == which)
            def _():
                for copy in copies(which):
                    copy.start()

    for which in range(2):
        for copy in copies(which):
            copy.wait()


def local(raw_strain, fir_taps, source_channels, live_counts):
    taps = fir_taps[None, :]
    src = source_channels[None, :]
    any_spec = pl.BlockSpec(memory_space=pl.ANY)
    vmem = pl.BlockSpec(memory_space=pltpu.VMEM)
    hbm = pl.BlockSpec(memory_space=pltpu.HBM)
    dma = pltpu.SemaphoreType.DMA
    heights = [rows for _, rows in PARTS]
    hops = NX - 1 + NY - 1 + NZ - 1
    blocks = NX + NY + NZ
    a, b, c, white = pl.pallas_call(
        gather_kernel,
        out_shape=(
            pltpu.VMEM((NC, NZ, NY, NX, heights[0], 128), BF16),
            pltpu.VMEM((NC, NX, NZ, NY, heights[1], 128), BF16),
            pltpu.VMEM((NC, NY, NX, NZ, heights[2], 128), BF16),
            pltpu.VMEM((KG, 16 * NSEG, 128), F32),
        ),
        in_specs=[hbm, vmem, vmem, pl.BlockSpec(memory_space=pltpu.SMEM), hbm],
        out_specs=(vmem, vmem, vmem, vmem),
        scratch_shapes=[
            pltpu.VMEM((256, 5248), BF16),
            pltpu.VMEM((256, REACH), BF16),
            pltpu.VMEM((256, HALF + 128), BF16),
            pltpu.VMEM((2, 16, HALF + 128), BF16),
            pltpu.VMEM((16, HALF + 128), BF16),
            pltpu.VMEM((2, 16, 128), BF16),
            pltpu.VMEM((TM, 16, HALF + 128), BF16),
            pltpu.VMEM((HALF, 2 * SEG), BF16),
            pltpu.VMEM((KG, 16, 128), BF16),
            pltpu.VMEM((32, 16, 128), BF16),
            pltpu.VMEM((SRC, 128), jnp.int32),
            pltpu.VMEM((QUOTA, 128), BF16),
            dma((4,)),
            dma,
            dma((2, 2)),
            dma((2,)),
            dma((TM - 1,)),
            dma((TM - 1,)),
            dma((hops,)),
            dma((hops,)),
            dma((hops,)),
            dma((hops,)),
            dma((hops,)),
            dma((hops,)),
            dma((3,)),
            dma((blocks,)),
            dma((blocks,)),
            dma((31,)),
            dma((31,)),
        ],
        compiler_params=pltpu.CompilerParams(
            collective_id=0, has_side_effects=True, vmem_limit_bytes=58 * 1024 * 1024
        ),
        name="filter_and_gather",
    )(raw_strain, taps, src, live_counts, jnp.asarray(dft_table()))
    return pl.pallas_call(
        correlate_kernel,
        out_shape=jax.ShapeDtypeStruct((SRC, 16, 2 * LAGH), F32),
        in_specs=[vmem, vmem, vmem, vmem, vmem],
        out_specs=any_spec,
        scratch_shapes=[
            pltpu.VMEM((SRC, NSEG * SEG), BF16),
            pltpu.VMEM((2, 256, 256), BF16),
            pltpu.VMEM((8, SRC, SEG), BF16),
            pltpu.VMEM((2, 3, SRC * 8, 128), F32),
            dma((2, 3)),
        ],
        compiler_params=pltpu.CompilerParams(vmem_limit_bytes=36 * 1024 * 1024),
        name="correlate",
    )(white.reshape(KG, 16, NSEG, 128), a, b, c, jnp.asarray(lag_table()))


def solution(mesh):
    placed = (P("chan", "tm"), P(), P(), P(("chan", "tm")))
    return jax.shard_map(
        local, mesh=mesh, in_specs=placed, out_specs=P(None, ("chan", "tm"), None), check_vma=False
    )
```

```python
import functools
import math

import jax
import jax.numpy as jnp
import numpy as np
from jax import lax
from jax.experimental import pallas as pl
from jax.experimental.pallas import tpu as pltpu
from jax.sharding import PartitionSpec as P

NX, NY, NZ, NC = 4, 4, 8, 2
TM, CHAN = 16, 16
DECIM, SEG, BAND, LAGH = 10, 1024, 64, 192
NSEG = 8
HALF = SEG // 2
SRC = 256
SLOTS = 512
EPS = 1e-06
MESH = pl.DeviceIdType.MESH
F32, BF16 = jnp.float32, jnp.bfloat16
TAPS = 128
REACH = 1408
KG = HALF // BAND
EDGE = 16
QUARTERS, BINS = 4, 16
QUOTA = SRC // NX
PARTS = ((0, 16), (16, 16), (32, 16), (48, 16))
ROUNDS = "ABCDACDBAACBADABCDABACBCADAD"
CUTS = (2, 2, 2, 2)


def dot(a, b):
    return jnp.dot(a, b, preferred_element_type=F32)


def hi_lo(table):
    hi = table.astype(np.float32).astype(jnp.bfloat16)
    lo = (table - hi.astype(np.float64)).astype(np.float32).astype(jnp.bfloat16)
    return hi, lo


def dft_table():
    n = np.arange(HALF)[:, None]
    k = np.arange(HALF)[None, :]
    phase = (n * k % SEG) * (2.0 * np.pi / SEG)
    both = np.stack([np.cos(phase), -np.sin(phase)], axis=1).reshape(HALF, 2, KG, QUARTERS, BINS)
    table = both.transpose(0, 2, 3, 1, 4).reshape(HALF, SEG)
    return np.concatenate(hi_lo(table), axis=1)


def lag_table():
    k = np.arange(HALF)[:, None]
    t = np.arange(-LAGH, LAGH)[None, :]
    phase = (k * t % SEG) * (2.0 * np.pi / SEG)
    weight = np.where(k == 0, 1.0, 2.0) * (math.sqrt(SEG / NSEG) / SEG)
    both = np.stack([weight * np.cos(phase), -weight * np.sin(phase)], axis=0)
    table = both.reshape(2, KG, QUARTERS, BINS, 2 * LAGH).transpose(1, 2, 0, 3, 4).reshape(SEG, 2 * LAGH)
    return table.astype(np.float32).astype(jnp.bfloat16)


def whiten(spec, turn=None):
    bands = []
    for band in range(KG):
        block = spec[:, band * 128 : (band + 1) * 128]
        power = jnp.sum(block * block, axis=1, keepdims=True) * (1.0 / BAND)
        block = block * lax.rsqrt(power + EPS)
        bands.append(block if turn is None else pltpu.roll(block, turn, 1))
    return jnp.concatenate(bands, axis=1).astype(BF16)


def odd_sign(rows):
    lane = lax.broadcasted_iota(jnp.int32, (rows, SEG), 1)
    return (1 - 2 * lax.rem(lane, 2)).astype(F32)


def place(x, y, z, core):
    return (y * 4 + z // 2, lax.rem(z, 2) * 8 + x * 2 + core)


def gather_part(semaphores, order, step_dir, sends, first, cuts):
    send_sem, recv_sem = semaphores
    count = 0
    for stage, (me, size, chunk, device) in enumerate(order):

        def index(offset):
            return lax.rem(me + step_dir * offset + size, size)

        def copy_of(src, to, number):
            return pltpu.make_async_remote_copy(
                src_ref=src[0],
                dst_ref=src[1],
                send_sem=send_sem.at[number],
                recv_sem=recv_sem.at[number],
                device_id=device(index(to)),
                device_id_type=MESH,
            )

        def send(src, dst, to, number):
            copy = copy_of((src, dst), to, number)
            copy.start()
            sends.append(copy)

        def arrived(offset, number):
            block = chunk(index(offset))
            copy_of((block, block), 1, number).wait_recv()
            return block

        own = chunk(me)
        start = first if stage == 0 else own
        if stage < len(order) - 1:
            for offset in range(1, size):
                send(start, own, offset, count + offset - 1)
            yield None
            for offset in range(1, size):
                arrived(-offset, count + offset - 1)
            count += size - 1
            continue
        far, near = size // 2, size - 1 - size // 2

        def piece(index, cut):
            block = chunk(index)
            depth = block.shape[0] // cuts
            return block.at[cut * depth : (cut + 1) * depth]

        def arrived_piece(offset, number, cut):
            block = piece(index(offset), cut)
            copy_of((block, block), 1, number).wait_recv()
            return block

        def number_of(hop, cut):
            return count + hop * cuts + cut

        for cut in range(cuts):
            own = piece(me, cut)
            send(own, own, 1, number_of(0, cut))
            send(own, own, -1, number_of(far, cut))
        for cut in range(cuts):
            yield piece(me, cut)
        for hop in range(1, far + 1):
            for cut in range(cuts):
                yield None
                block = arrived_piece(-hop, number_of(hop - 1, cut), cut)
                if hop < far:
                    send(block, block, 1, number_of(hop, cut))
                yield block
                if hop <= near:
                    block = arrived_piece(hop, number_of(far + hop - 1, cut), cut)
                    if hop < near:
                        send(block, block, -1, number_of(far + hop, cut))
                    yield block


def gather_kernel(
    raw_hbm, taps_ref, src_ref, live_ref, table_hbm,
    a_ref, b_ref, c_ref, d_ref, white_ref,
    raw_v, tap_v, dec_v, sel_v, pair_v, edge_v, trace_v, table_v, own_v, slot_v, place_v, block_v,
    load_sem, table_sem, halo_sem, pair_sem, trace_send, trace_recv,
    a_send, a_recv, b_send, b_recv, c_send, c_recv, d_send, d_recv, own_sem, twin_send, twin_recv, spread_send, spread_recv,
):
    tm = lax.axis_index("tm")
    chan = lax.axis_index("chan")
    y, z_hi = tm // 4, lax.rem(tm, 4)
    z_lo, x, core = chan // 8, lax.rem(chan, 8) // 2, lax.rem(chan, 2)
    z = z_hi * 2 + z_lo
    direction = 1 - 2 * core
    half = lax.rem(tm, 2)

    def remote(src, dst, sems, device):
        return pltpu.make_async_remote_copy(
            src_ref=src, dst_ref=dst, send_sem=sems[0], recv_sem=sems[1], device_id=device, device_id_type=MESH
        )

    loads = []
    for part in range(4):
        loads.append(
            pltpu.make_async_copy(
                raw_hbm.at[:, part * 1280 : (part + 1) * 1280],
                raw_v.at[:, 128 + part * 1280 : 128 + (part + 1) * 1280],
                load_sem.at[part],
            )
        )
        loads[-1].start()
    table_load = pltpu.make_async_copy(table_hbm, table_v, table_sem)
    table_load.start()

    barrier = pltpu.get_barrier_semaphore()
    peers = [(lax.rem(tm + step, TM), chan) for step in range(1, TM)]
    twin = place(x, y, z, 1 - core)
    run = lax.rem(z, 4)
    spread = []
    for step in range(1, 32):
        to_run = lax.rem(run + step // 8, 4)
        to_x = lax.rem(x + step // 2, NX)
        to_core = lax.rem(core + step, NC)
        spread.append((place(to_x, y, z - run + to_run, to_core), to_run * 2 + to_core))
        peers.append(spread[-1][0])
    for step in (1, 3, 5, 7):
        peers.append(place(x, y, lax.rem(z + step, NZ), core))
    for peer in peers:
        pl.semaphore_signal(barrier, inc=1, device_id=peer, device_id_type=MESH)
    taps_col = jnp.transpose(jnp.broadcast_to(taps_ref[...], (TAPS, TAPS)))
    tap_row = lax.broadcasted_iota(jnp.int32, (TAPS, 384), 0)
    tap_lane = lax.broadcasted_iota(jnp.int32, (TAPS, 384), 1)
    taps_wide = jnp.concatenate([taps_col] * 3, axis=1)
    rev = jnp.sum(jnp.where(tap_row + tap_lane == TAPS, taps_wide, 0.0), axis=0, keepdims=True)
    base = pltpu.roll(jnp.broadcast_to(rev, (8, 384)), 0, 1, stride=DECIM, stride_axis=0)
    for group in range(8):
        rows = []
        for octet in (2 * group, 2 * group + 1):
            at, turn = divmod(octet * 8 * DECIM, 128)
            piece = pltpu.roll(base, turn, 1) if turn else base
            blocks = [jnp.zeros((8, 128), F32)] * (REACH // 128)
            for number in range(min(3, REACH // 128 - at)):
                blocks[at + number] = piece[:, number * 128 : (number + 1) * 128]
            rows.append(jnp.concatenate(blocks, axis=1))
        band = jnp.concatenate(rows, axis=0)
        band_hi = band.astype(BF16)
        tap_v[group * 16 : group * 16 + 16, :] = band_hi
        tap_v[128 + group * 16 : 128 + group * 16 + 16, :] = (band - band_hi.astype(F32)).astype(BF16)

    src = src_ref[...].astype(F32)
    src_col = jnp.transpose(jnp.broadcast_to(src, (SRC, SRC)))
    lane = lax.broadcasted_iota(jnp.int32, (SRC, SRC), 1)
    row = lax.broadcasted_iota(jnp.int32, (SRC, SRC), 0)
    hit = jnp.where(src_col == (lane + chan * 256).astype(F32), 1.0, 0.0)
    is_src = jnp.sum(hit, axis=0, keepdims=True)
    earlier = jnp.where((row // 16 == lane // 16) & (row < lane), 1.0, 0.0)
    rank = dot(jnp.broadcast_to(is_src, (16, SRC)).astype(BF16), earlier.astype(BF16))[0:1, :]
    pick_row = lax.broadcasted_iota(jnp.int32, (32, SRC), 0)
    pick_lane = lax.broadcasted_iota(jnp.int32, (32, SRC), 1)
    pick = jnp.where(
        (pick_row // 2 == pick_lane // 16) & (lax.rem(pick_row, 2).astype(F32) == rank) & (is_src > 0.5), 1.0, 0.0
    ).astype(BF16)

    src_row = jnp.broadcast_to(src, (SRC, SRC))
    row_block = jnp.floor(src_row * (1.0 / 16))
    col_block = jnp.floor(src_col * (1.0 / 16))
    before = jnp.where((row_block == col_block) & (src_row < src_col), 1.0, 0.0)
    behind = jnp.sum(before, axis=1, keepdims=True).astype(jnp.int32)
    block_of = col_block[:, 0:1].astype(jnp.int32)
    chan_of, local_of = block_of // 16, lax.rem(block_of, 16)
    spot = ((local_of // 8) * 2 + chan_of // 8) * 128 + lax.rem(chan_of, 8) * 16 + 2 * lax.rem(local_of, 8) + behind
    place_v[...] = jnp.broadcast_to(spot, (SRC, 128))

    def filtered(samples, taps):
        both = lax.dot_general(samples, taps, (((1,), (1,)), ((), ())), preferred_element_type=F32)
        return both[:, 0:128] + both[:, 128:256]

    raw_v[:, 0:128] = jnp.zeros((256, 128), BF16)
    heads = None
    for part in range(4):
        loads[part].wait()
        sums = filtered(raw_v[:, part * 1280 : part * 1280 + REACH], tap_v[...])
        dec_v[:, part * 128 : (part + 1) * 128] = sums.astype(BF16)
        heads = sums if part == 0 else heads
    tails = filtered(raw_v[:, 5120:5248], tap_v[:, 0:128])
    edge_lane = lax.broadcasted_iota(jnp.int32, (256, 128), 1)
    edge = jnp.where(edge_lane < 64, heads, pltpu.roll(tails, 64, 1))
    edge = jnp.where(lax.rem(edge_lane, 64) < EDGE, edge, 0.0)
    packed = jnp.zeros((256, 128), F32)
    for number in range(3):
        piece = edge.astype(BF16).astype(F32)
        edge = edge - piece
        packed = packed + (pltpu.roll(piece, number * EDGE, 1) if number else piece)
    dec_v[:, HALF:] = packed.astype(BF16)

    def joined(main, edges, before):
        def whole(rows, at):
            full = pltpu.roll(rows, 128 - at, 1) if at else rows
            for number in (1, 2):
                full = full + pltpu.roll(rows, 128 - at - number * EDGE, 1)
            return full

        sums = (whole(edges.astype(F32), 0) + whole(before.astype(F32), 64)).astype(BF16)
        lanes = lax.broadcasted_iota(jnp.int32, sums.shape, 1)
        first = jnp.where(lanes < EDGE, sums.astype(F32), main[:, 0:128].astype(F32)).astype(BF16)
        return jnp.concatenate([first, main[:, 128:]], axis=1)

    picked = dot(pick, dec_v[...]).astype(BF16)
    sel_v[0] = picked[0:16]
    sel_v[1] = picked[16:32]
    pl.semaphore_wait(barrier, len(peers))
    pair = remote(sel_v.at[1 - half], pair_v, (pair_sem.at[0], pair_sem.at[1]), (tm + 1 - 2 * half, chan))
    pair.start()
    edge_copies = []
    for step in (1, 2):
        copy = remote(
            sel_v.at[(1 - half) if step == 1 else half, :, HALF:],
            edge_v.at[step - 1],
            (halo_sem.at[0, step - 1], halo_sem.at[1, step - 1]),
            (lax.rem(tm + step, TM), chan),
        )
        copy.start()
        edge_copies.append(copy)

    pair.wait()
    for copy in edge_copies:
        copy.wait()
    table_load.wait()
    is_first = half == 0
    mine, other = sel_v[half].astype(F32), pair_v[...].astype(F32)
    low, high = jnp.where(is_first, mine, other), jnp.where(is_first, other, mine)
    tail = jnp.where(is_first, edge_v[0].astype(F32), edge_v[1].astype(F32))
    tail = jnp.where(tm // 2 == 0, 0.0, tail)
    low_edge, high_edge = low[:, HALF:], high[:, HALF:]
    low = joined(low[:, 0:HALF].astype(BF16), low_edge, tail)
    high = joined(high[:, 0:HALF].astype(BF16), high_edge, low_edge)
    spec = dot(jnp.concatenate([low, high], axis=0), table_v[...])
    sign = odd_sign(16)
    full = whiten(
        spec[0:16, 0:SEG] + spec[0:16, SEG:] + sign * (spec[16:32, 0:SEG] + spec[16:32, SEG:]),
        32 * lax.rem(tm // 2, 4),
    )
    for band in range(KG):
        own_v[band] = full[:, band * 128 : (band + 1) * 128]

    here = run * 8 + x * 2 + core
    spreads = []
    for number, (peer, band) in enumerate(spread):
        copy = remote(own_v.at[band], slot_v.at[here], (spread_send.at[number], spread_recv.at[number]), peer)
        copy.start()
        spreads.append(copy)
    slot_v[here] = own_v[run * 2 + core]

    traces = []
    for step in range(1, TM):
        to = lax.rem(tm + step, TM)
        copy = remote(
            dec_v.at[pl.ds(pl.multiple_of(to * 16, 16), 16), :],
            trace_v.at[tm],
            (trace_send.at[step - 1], trace_recv.at[step - 1]),
            (to, chan),
        )
        copy.start()
        traces.append(copy)
    trace_v[tm] = dec_v[pl.ds(pl.multiple_of(tm * 16, 16), 16), :]
    wanted = place_v[pl.ds(pl.multiple_of(x * QUOTA, QUOTA), QUOTA), :]
    slot_lane = lax.broadcasted_iota(jnp.int32, (QUOTA, 128), 1)
    chosen = jnp.concatenate(
        [jnp.where(wanted == slot_lane + part * 128, 1.0, 0.0) for part in range(SLOTS // 128)], axis=1
    ).astype(BF16)
    for copy in spreads:
        copy.wait()
    block_v[...] = dot(chosen, slot_v[...].reshape(SLOTS, 128)).astype(BF16)

    def part_order(buf, axes):
        sizes = {"x": NX, "y": NY, "z": NZ}
        at = {"x": x, "y": y, "z": z}
        order = []
        for number, axis in enumerate(axes):
            lead = [at[a] for a in reversed(axes[number + 1 :])]

            def chunk(index, lead=lead):
                return buf.at[(core, *lead, index)]

            def device(index, axis=axis):
                where = dict(at)
                where[axis] = index
                return place(where["x"], where["y"], where["z"], core)

            order.append((at[axis], sizes[axis], chunk, device))
        return order

    sends = []
    routines = []
    own_copies = []
    bufs = (
        (a_ref, "xyz", a_send, a_recv),
        (b_ref, "yzx", b_send, b_recv),
        (c_ref, "zxy", c_send, c_recv),
        (d_ref, "zxy", d_send, d_recv),
    )
    for number, (buf, axes, send_sem, recv_sem) in enumerate(bufs):
        begin, rows = PARTS[number]
        first = block_v.at[begin : begin + rows]
        at = {"x": x, "y": y, "z": z}
        slot = buf.at[(core, *(at[a] for a in reversed(axes)))]
        copy = pltpu.make_async_copy(first, slot, own_sem.at[number])
        copy.start()
        own_copies.append(copy)
        order = part_order(buf, axes)
        routines.append(gather_part((send_sem, recv_sem), order, direction, sends, first, CUTS[number]))

    twins = []

    def to_twin(block):
        number = len(twins)
        copy = remote(block, block, (twin_send.at[number], twin_recv.at[number]), twin)
        copy.start()
        twins.append(copy)

    def advance(name):
        for block in routines["ABCD".index(name)]:
            if block is None:
                break
            to_twin(block)

    def own_channels(part):
        rows = lax.broadcasted_iota(jnp.int32, (128, HALF), 0)
        alive = lax.rem(rows, 16) < live_ref[0]
        main = trace_v[part * 8 : part * 8 + 8, :, 0:HALF].reshape(128, HALF)
        edges = trace_v[part * 8 : part * 8 + 8, :, HALF:].reshape(128, 128).astype(F32)
        if part:
            before = trace_v[part * 8 - 1, :, HALF:].astype(F32)
        else:
            before = jnp.zeros((16, 128), F32)
        flat = joined(main, edges, jnp.concatenate([before, edges[0:112]], axis=0))
        spec = dot(jnp.where(alive, flat, jnp.zeros_like(flat)), table_v[...])
        for seg in range(NSEG // 2):
            low = spec[seg * 32 : seg * 32 + 16]
            high = spec[seg * 32 + 16 : seg * 32 + 32]
            full = low[:, 0:SEG] + low[:, SEG:] + sign * (high[:, 0:SEG] + high[:, SEG:])
            white = whiten(full).astype(F32)
            for band in range(KG):
                rows_at = pl.ds(part * 4 + seg, 16, stride=NSEG)
                white_ref[band, rows_at, :] = white[:, band * 128 : (band + 1) * 128]

    for name in "ABCD":
        advance(name)
    for copy in own_copies:
        copy.wait()
    for copy in traces:
        copy.wait()
    own_channels(0)
    for number, name in enumerate(ROUNDS):
        if number == 5:
            own_channels(1)
        advance(name)
    for copy in sends:
        copy.wait_send()
    for copy in twins:
        copy.wait()


def correlate_kernel(white_ref, a_ref, b_ref, c_ref, d_ref, lag_ref, out_hbm, all_v, weight_v, cross_v, out_v, out_sem):
    quarter = lax.broadcasted_iota(jnp.int32, (SRC, 128), 1) // 32
    quarter_b = quarter.astype(F32).astype(BF16)

    def merge(blocks, shift, rows=16):
        lanes = (quarter_b if blocks[0].dtype == BF16 else quarter)[0:rows]
        masks = [lanes == j for j in range(4)]
        pieces = []
        for at in range(0, blocks[0].shape[0], rows):
            full = blocks[(0 - shift) % 4][at : at + rows]
            for j in range(1, 4):
                full = jnp.where(masks[j], blocks[(j - shift) % 4][at : at + rows], full)
            pieces.append(full)
        return jnp.concatenate(pieces, axis=0) if len(pieces) > 1 else pieces[0]

    for band in range(KG):
        run, core = band // 2, band % 2
        for four in range(2):
            blocks = []
            for seg in range(four * 4, four * 4 + 4):
                y, z = seg // 2, (seg % 2) * 4 + run
                pieces = []
                for x in range(NX):
                    pieces += [a_ref[core, z, y, x], b_ref[core, x, z, y], c_ref[core, y, x, z], d_ref[core, y, x, z]]
                blocks.append(jnp.concatenate(pieces, axis=0))
            for part in range(QUARTERS):
                lane = ((band * QUARTERS + part) * 2 + four) * 128
                all_v[:, lane : lane + 128] = merge(blocks, part)

    row = lax.broadcasted_iota(jnp.int32, (BINS, 128), 0)
    lane = lax.broadcasted_iota(jnp.int32, (BINS, 128), 1)
    same = row.astype(F32).astype(BF16) == lax.rem(lane, BINS).astype(F32).astype(BF16)

    def spread(rows, seg):
        wide = jnp.broadcast_to(rows[seg : seg + 1], (BINS, 128)).astype(BF16)
        return jnp.where(same, wide, jnp.zeros_like(wide))

    is_re = lax.rem(lane[0:8], 2 * BINS) < BINS

    def copies(which):
        return [
            pltpu.make_async_copy(
                out_v.at[which, part].reshape(SRC, 8, 128),
                out_hbm.at[:, which * 8 : which * 8 + 8, part * 128 : (part + 1) * 128],
                out_sem.at[which, part],
            )
            for part in range(3)
        ]

    @pl.loop(0, 2)
    def _(octet):
        @pl.loop(0, 4)
        def _(band_pair):
          for sub in range(2):
            band = band_pair * 2 + sub
            crosses = []
            turned = [pltpu.roll(white_ref[band, 8 * octet + c], 32 * (c % 4), 1) if c % 4 else white_ref[band, 8 * octet + c] for c in range(8)]
            for part in range(QUARTERS):
                slot = part % 2
                for group in range(2):
                    v = merge(turned[group * 4 : group * 4 + 4], part, 8)
                    u = jnp.where(is_re, pltpu.roll(v, 128 - BINS, 1), -pltpu.roll(v, BINS, 1))
                    lanes = slice(group * 128, group * 128 + 128)
                    for four in range(2):
                        for j in range(4):
                            seg = four * 4 + (j - part) % 4
                            at = four * 128 + j * 32
                            weight_v[slot, at : at + 16, lanes] = spread(v, seg)
                            weight_v[slot, at + 16 : at + 32, lanes] = spread(u, seg)
                at = pl.multiple_of((band * QUARTERS + part) * 256, 256)
                crosses.append(dot(all_v[:, pl.ds(at, 256)], weight_v[slot]).astype(BF16))
            for c in range(8):
                blocks = [cross[:, c // 4 * 128 : c // 4 * 128 + 128] for cross in crosses]
                full = merge(blocks, c)
                cross_v[c, :, pl.ds(pl.multiple_of(band * 128, 128), 128)] = full
        @pl.loop(0, 2)
        def _(four):
            for c in range(4):
                table = jnp.concatenate(
                    [
                        lag_ref[band * 128 + (j - c) % 4 * 32 : band * 128 + (j - c) % 4 * 32 + 32, :]
                        for band in range(KG)
                        for j in range(4)
                    ],
                    axis=0,
                )
                lags = dot(cross_v[four * 4 + c], table)
                for part in range(3):
                    out_v[octet, part, pl.ds(four * 4 + c, SRC, stride=8), :] = lags[:, part * 128 : (part + 1) * 128]

        for which in range(2):

            @pl.when(octet == which)
            def _():
                for copy in copies(which):
                    copy.start()

    for which in range(2):
        for copy in copies(which):
            copy.wait()


def local(raw_strain, fir_taps, source_channels, live_counts):
    taps = fir_taps[None, :]
    src = source_channels[None, :]
    any_spec = pl.BlockSpec(memory_space=pl.ANY)
    vmem = pl.BlockSpec(memory_space=pltpu.VMEM)
    hbm = pl.BlockSpec(memory_space=pltpu.HBM)
    dma = pltpu.SemaphoreType.DMA
    heights = [rows for _, rows in PARTS]
    early = (NX + NY - 2, NY + NZ - 2, NZ + NX - 2, NZ + NX - 2)
    last = (NZ, NX, NY, NY)
    hops = [start + (size - 1) * cuts for start, size, cuts in zip(early, last, CUTS)]
    blocks = sum(size * cuts for size, cuts in zip(last, CUTS))
    a, b, c, d, white = pl.pallas_call(
        gather_kernel,
        out_shape=(
            pltpu.VMEM((NC, NZ, NY, NX, heights[0], 128), BF16),
            pltpu.VMEM((NC, NX, NZ, NY, heights[1], 128), BF16),
            pltpu.VMEM((NC, NY, NX, NZ, heights[2], 128), BF16),
            pltpu.VMEM((NC, NY, NX, NZ, heights[3], 128), BF16),
            pltpu.VMEM((KG, 16 * NSEG, 128), F32),
        ),
        in_specs=[hbm, vmem, vmem, pl.BlockSpec(memory_space=pltpu.SMEM), hbm],
        out_specs=(vmem, vmem, vmem, vmem, vmem),
        scratch_shapes=[
            pltpu.VMEM((256, 5248), BF16),
            pltpu.VMEM((256, REACH), BF16),
            pltpu.VMEM((256, HALF + 128), BF16),
            pltpu.VMEM((2, 16, HALF + 128), BF16),
            pltpu.VMEM((16, HALF + 128), BF16),
            pltpu.VMEM((2, 16, 128), BF16),
            pltpu.VMEM((TM, 16, HALF + 128), BF16),
            pltpu.VMEM((HALF, 2 * SEG), BF16),
            pltpu.VMEM((KG, 16, 128), BF16),
            pltpu.VMEM((32, 16, 128), BF16),
            pltpu.VMEM((SRC, 128), jnp.int32),
            pltpu.VMEM((QUOTA, 128), BF16),
            dma((4,)),
            dma,
            dma((2, 2)),
            dma((2,)),
            dma((TM - 1,)),
            dma((TM - 1,)),
            *(dma((count,)) for count in hops for _ in range(2)),
            dma((4,)),
            dma((blocks,)),
            dma((blocks,)),
            dma((31,)),
            dma((31,)),
        ],
        compiler_params=pltpu.CompilerParams(
            collective_id=0, has_side_effects=True, vmem_limit_bytes=58 * 1024 * 1024
        ),
        name="filter_and_gather",
    )(raw_strain, taps, src, live_counts, jnp.asarray(dft_table()))
    return pl.pallas_call(
        correlate_kernel,
        out_shape=jax.ShapeDtypeStruct((SRC, 16, 2 * LAGH), F32),
        in_specs=[vmem, vmem, vmem, vmem, vmem, vmem],
        out_specs=any_spec,
        scratch_shapes=[
            pltpu.VMEM((SRC, NSEG * SEG), BF16),
            pltpu.VMEM((2, 256, 256), BF16),
            pltpu.VMEM((8, SRC, SEG), BF16),
            pltpu.VMEM((2, 3, SRC * 8, 128), F32),
            dma((2, 3)),
        ],
        compiler_params=pltpu.CompilerParams(vmem_limit_bytes=36 * 1024 * 1024),
        name="correlate",
    )(white.reshape(KG, 16, NSEG, 128), a, b, c, d, jnp.asarray(lag_table()))


def solution(mesh):
    placed = (P("chan", "tm"), P(), P(), P(("chan", "tm")))
    return jax.shard_map(
        local, mesh=mesh, in_specs=placed, out_specs=P(None, ("chan", "tm"), None), check_vma=False
    )
```

```python
import functools
import math

import jax
import jax.numpy as jnp
import numpy as np
from jax import lax
from jax.experimental import pallas as pl
from jax.experimental.pallas import tpu as pltpu
from jax.sharding import PartitionSpec as P

NX, NY, NZ, NC = 4, 4, 8, 2
TM, CHAN = 16, 16
DECIM, SEG, BAND, LAGH = 10, 1024, 64, 192
NSEG = 8
HALF = SEG // 2
SRC = 256
SLOTS = 512
EPS = 1e-06
MESH = pl.DeviceIdType.MESH
F32, BF16 = jnp.float32, jnp.bfloat16
TAPS = 128
REACH = 1408
KG = HALF // BAND
EDGE = 16
QUARTERS, BINS = 4, 16
QUOTA = SRC // NX
PARTS = ((0, 16), (16, 16), (32, 16), (48, 16))
ROUNDS = "ABCDACDBAACBADABCDABACBCADAD"
CUTS = (2, 2, 2, 2)


def dot(a, b):
    return jnp.dot(a, b, preferred_element_type=F32)


def hi_lo(table):
    hi = table.astype(np.float32).astype(jnp.bfloat16)
    lo = (table - hi.astype(np.float64)).astype(np.float32).astype(jnp.bfloat16)
    return hi, lo


def dft_table():
    n = np.arange(HALF)[:, None]
    k = np.arange(HALF)[None, :]
    phase = (n * k % SEG) * (2.0 * np.pi / SEG)
    both = np.stack([np.cos(phase), -np.sin(phase)], axis=1).reshape(HALF, 2, KG, QUARTERS, BINS)
    table = both.transpose(0, 2, 3, 1, 4).reshape(HALF, SEG)
    return np.concatenate(hi_lo(table), axis=1)


def lag_table():
    k = np.arange(HALF)[:, None]
    t = np.arange(-LAGH, LAGH)[None, :]
    phase = (k * t % SEG) * (2.0 * np.pi / SEG)
    weight = np.where(k == 0, 1.0, 2.0) * (math.sqrt(SEG / NSEG) / SEG)
    both = np.stack([weight * np.cos(phase), -weight * np.sin(phase)], axis=0)
    table = both.reshape(2, KG, QUARTERS, BINS, 2 * LAGH).transpose(1, 2, 0, 3, 4).reshape(SEG, 2 * LAGH)
    return table.astype(np.float32).astype(jnp.bfloat16)


def whiten(spec, turn=None):
    bands = []
    for band in range(KG):
        block = spec[:, band * 128 : (band + 1) * 128]
        power = jnp.sum(block * block, axis=1, keepdims=True) * (1.0 / BAND)
        block = block * lax.rsqrt(power + EPS)
        bands.append(block if turn is None else pltpu.roll(block, turn, 1))
    return jnp.concatenate(bands, axis=1).astype(BF16)


def odd_sign(rows):
    lane = lax.broadcasted_iota(jnp.int32, (rows, SEG), 1)
    return (1 - 2 * lax.rem(lane, 2)).astype(F32)


def place(x, y, z, core):
    return (y * 4 + z // 2, lax.rem(z, 2) * 8 + x * 2 + core)


def gather_part(semaphores, order, step_dir, sends, first, cuts):
    send_sem, recv_sem = semaphores
    count = 0
    for stage, (me, size, chunk, device) in enumerate(order):

        def index(offset):
            return lax.rem(me + step_dir * offset + size, size)

        def copy_of(src, to, number):
            return pltpu.make_async_remote_copy(
                src_ref=src[0],
                dst_ref=src[1],
                send_sem=send_sem.at[number],
                recv_sem=recv_sem.at[number],
                device_id=device(index(to)),
                device_id_type=MESH,
            )

        def send(src, dst, to, number):
            copy = copy_of((src, dst), to, number)
            copy.start()
            sends.append(copy)

        def arrived(offset, number):
            block = chunk(index(offset))
            copy_of((block, block), 1, number).wait_recv()
            return block

        own = chunk(me)
        start = first if stage == 0 else own
        if stage < len(order) - 1:
            for offset in range(1, size):
                send(start, own, offset, count + offset - 1)
            yield None
            for offset in range(1, size):
                arrived(-offset, count + offset - 1)
            count += size - 1
            continue
        far, near = size // 2, size - 1 - size // 2

        def piece(index, cut):
            block = chunk(index)
            depth = block.shape[0] // cuts
            return block.at[cut * depth : (cut + 1) * depth]

        def arrived_piece(offset, number, cut):
            block = piece(index(offset), cut)
            copy_of((block, block), 1, number).wait_recv()
            return block

        def number_of(hop, cut):
            return count + hop * cuts + cut

        for cut in range(cuts):
            own = piece(me, cut)
            send(own, own, 1, number_of(0, cut))
            send(own, own, -1, number_of(far, cut))
        for cut in range(cuts):
            yield piece(me, cut)
        for hop in range(1, far + 1):
            for cut in range(cuts):
                yield None
                block = arrived_piece(-hop, number_of(hop - 1, cut), cut)
                if hop < far:
                    send(block, block, 1, number_of(hop, cut))
                yield block
                if hop <= near:
                    block = arrived_piece(hop, number_of(far + hop - 1, cut), cut)
                    if hop < near:
                        send(block, block, -1, number_of(far + hop, cut))
                    yield block


def gather_kernel(
    raw_hbm, taps_ref, src_ref, live_ref, table_hbm,
    a_ref, b_ref, c_ref, d_ref, white_ref,
    raw_v, tap_v, dec_v, sel_v, pair_v, edge_v, trace_v, table_v, own_v, slot_v, place_v, block_v,
    load_sem, table_sem, halo_sem, pair_sem, trace_send, trace_recv,
    a_send, a_recv, b_send, b_recv, c_send, c_recv, d_send, d_recv, own_sem, twin_send, twin_recv, spread_send, spread_recv,
):
    tm = lax.axis_index("tm")
    chan = lax.axis_index("chan")
    y, z_hi = tm // 4, lax.rem(tm, 4)
    z_lo, x, core = chan // 8, lax.rem(chan, 8) // 2, lax.rem(chan, 2)
    z = z_hi * 2 + z_lo
    direction = 1 - 2 * core
    half = lax.rem(tm, 2)

    def remote(src, dst, sems, device):
        return pltpu.make_async_remote_copy(
            src_ref=src, dst_ref=dst, send_sem=sems[0], recv_sem=sems[1], device_id=device, device_id_type=MESH
        )

    loads = []
    for part in range(4):
        loads.append(
            pltpu.make_async_copy(
                raw_hbm.at[:, part * 1280 : (part + 1) * 1280],
                raw_v.at[:, 128 + part * 1280 : 128 + (part + 1) * 1280],
                load_sem.at[part],
            )
        )
        loads[-1].start()
    table_load = pltpu.make_async_copy(table_hbm, table_v, table_sem)
    table_load.start()

    barrier = pltpu.get_barrier_semaphore()
    peers = [(lax.rem(tm + step, TM), chan) for step in range(1, TM)]
    twin = place(x, y, z, 1 - core)
    run = lax.rem(z, 4)
    spread = []
    for step in range(1, 32):
        to_run = lax.rem(run + step // 8, 4)
        to_x = lax.rem(x + step // 2, NX)
        to_core = lax.rem(core + step, NC)
        spread.append((place(to_x, y, z - run + to_run, to_core), to_run * 2 + to_core))
        peers.append(spread[-1][0])
    for step in (1, 3, 5, 7):
        peers.append(place(x, y, lax.rem(z + step, NZ), core))
    for peer in peers:
        pl.semaphore_signal(barrier, inc=1, device_id=peer, device_id_type=MESH)
    taps_col = jnp.transpose(jnp.broadcast_to(taps_ref[...], (TAPS, TAPS)))
    tap_row = lax.broadcasted_iota(jnp.int32, (TAPS, 384), 0)
    tap_lane = lax.broadcasted_iota(jnp.int32, (TAPS, 384), 1)
    taps_wide = jnp.concatenate([taps_col] * 3, axis=1)
    rev = jnp.sum(jnp.where(tap_row + tap_lane == TAPS, taps_wide, 0.0), axis=0, keepdims=True)
    base = pltpu.roll(jnp.broadcast_to(rev, (8, 384)), 0, 1, stride=DECIM, stride_axis=0)
    for group in range(8):
        rows = []
        for octet in (2 * group, 2 * group + 1):
            at, turn = divmod(octet * 8 * DECIM, 128)
            piece = pltpu.roll(base, turn, 1) if turn else base
            blocks = [jnp.zeros((8, 128), F32)] * (REACH // 128)
            for number in range(min(3, REACH // 128 - at)):
                blocks[at + number] = piece[:, number * 128 : (number + 1) * 128]
            rows.append(jnp.concatenate(blocks, axis=1))
        band = jnp.concatenate(rows, axis=0)
        band_hi = band.astype(BF16)
        tap_v[group * 16 : group * 16 + 16, :] = band_hi
        tap_v[128 + group * 16 : 128 + group * 16 + 16, :] = (band - band_hi.astype(F32)).astype(BF16)

    src = src_ref[...].astype(F32)
    src_col = jnp.transpose(jnp.broadcast_to(src, (SRC, SRC)))
    lane = lax.broadcasted_iota(jnp.int32, (SRC, SRC), 1)
    row = lax.broadcasted_iota(jnp.int32, (SRC, SRC), 0)
    hit = jnp.where(src_col == (lane + chan * 256).astype(F32), 1.0, 0.0)
    is_src = jnp.sum(hit, axis=0, keepdims=True)
    earlier = jnp.where((row // 16 == lane // 16) & (row < lane), 1.0, 0.0)
    rank = dot(jnp.broadcast_to(is_src, (16, SRC)).astype(BF16), earlier.astype(BF16))[0:1, :]
    pick_row = lax.broadcasted_iota(jnp.int32, (32, SRC), 0)
    pick_lane = lax.broadcasted_iota(jnp.int32, (32, SRC), 1)
    pick = jnp.where(
        (pick_row // 2 == pick_lane // 16) & (lax.rem(pick_row, 2).astype(F32) == rank) & (is_src > 0.5), 1.0, 0.0
    ).astype(BF16)

    src_row = jnp.broadcast_to(src, (SRC, SRC))
    row_block = jnp.floor(src_row * (1.0 / 16))
    col_block = jnp.floor(src_col * (1.0 / 16))
    before = jnp.where((row_block == col_block) & (src_row < src_col), 1.0, 0.0)
    behind = jnp.sum(before, axis=1, keepdims=True).astype(jnp.int32)
    block_of = col_block[:, 0:1].astype(jnp.int32)
    chan_of, local_of = block_of // 16, lax.rem(block_of, 16)
    spot = ((local_of // 8) * 2 + chan_of // 8) * 128 + lax.rem(chan_of, 8) * 16 + 2 * lax.rem(local_of, 8) + behind
    place_v[...] = jnp.broadcast_to(spot, (SRC, 128))

    def filtered(samples, taps):
        both = lax.dot_general(samples, taps, (((1,), (1,)), ((), ())), preferred_element_type=F32)
        return both[:, 0:128] + both[:, 128:256]

    raw_v[:, 0:128] = jnp.zeros((256, 128), BF16)
    heads = None
    for part in range(4):
        loads[part].wait()
        sums = filtered(raw_v[:, part * 1280 : part * 1280 + REACH], tap_v[...])
        dec_v[:, part * 128 : (part + 1) * 128] = sums.astype(BF16)
        heads = sums if part == 0 else heads
    tails = filtered(raw_v[:, 5120:5248], tap_v[:, 0:128])
    edge_lane = lax.broadcasted_iota(jnp.int32, (256, 128), 1)
    edge = jnp.where(edge_lane < 64, heads, pltpu.roll(tails, 64, 1))
    edge = jnp.where(lax.rem(edge_lane, 64) < EDGE, edge, 0.0)
    packed = jnp.zeros((256, 128), F32)
    for number in range(3):
        piece = edge.astype(BF16).astype(F32)
        edge = edge - piece
        packed = packed + (pltpu.roll(piece, number * EDGE, 1) if number else piece)
    dec_v[:, HALF:] = packed.astype(BF16)

    def joined(main, edges, before):
        def whole(rows, at):
            full = pltpu.roll(rows, 128 - at, 1) if at else rows
            for number in (1, 2):
                full = full + pltpu.roll(rows, 128 - at - number * EDGE, 1)
            return full

        sums = (whole(edges.astype(F32), 0) + whole(before.astype(F32), 64)).astype(BF16)
        lanes = lax.broadcasted_iota(jnp.int32, sums.shape, 1)
        first = jnp.where(lanes < EDGE, sums.astype(F32), main[:, 0:128].astype(F32)).astype(BF16)
        return jnp.concatenate([first, main[:, 128:]], axis=1)

    picked = dot(pick, dec_v[...]).astype(BF16)
    sel_v[0] = picked[0:16]
    sel_v[1] = picked[16:32]
    pl.semaphore_wait(barrier, len(peers))
    pair = remote(sel_v.at[1 - half], pair_v, (pair_sem.at[0], pair_sem.at[1]), (tm + 1 - 2 * half, chan))
    pair.start()
    edge_copies = []
    for step in (1, 2):
        copy = remote(
            sel_v.at[(1 - half) if step == 1 else half, :, HALF:],
            edge_v.at[step - 1],
            (halo_sem.at[0, step - 1], halo_sem.at[1, step - 1]),
            (lax.rem(tm + step, TM), chan),
        )
        copy.start()
        edge_copies.append(copy)

    pair.wait()
    for copy in edge_copies:
        copy.wait()
    table_load.wait()
    is_first = half == 0
    mine, other = sel_v[half].astype(F32), pair_v[...].astype(F32)
    low, high = jnp.where(is_first, mine, other), jnp.where(is_first, other, mine)
    tail = jnp.where(is_first, edge_v[0].astype(F32), edge_v[1].astype(F32))
    tail = jnp.where(tm // 2 == 0, 0.0, tail)
    low_edge, high_edge = low[:, HALF:], high[:, HALF:]
    low = joined(low[:, 0:HALF].astype(BF16), low_edge, tail)
    high = joined(high[:, 0:HALF].astype(BF16), high_edge, low_edge)
    spec = dot(jnp.concatenate([low, high], axis=0), table_v[...])
    sign = odd_sign(16)
    full = whiten(
        spec[0:16, 0:SEG] + spec[0:16, SEG:] + sign * (spec[16:32, 0:SEG] + spec[16:32, SEG:]),
        32 * lax.rem(tm // 2, 4),
    )
    for band in range(KG):
        own_v[band] = full[:, band * 128 : (band + 1) * 128]

    here = run * 8 + x * 2 + core
    spreads = []
    for number, (peer, band) in enumerate(spread):
        copy = remote(own_v.at[band], slot_v.at[here], (spread_send.at[number], spread_recv.at[number]), peer)
        copy.start()
        spreads.append(copy)
    slot_v[here] = own_v[run * 2 + core]

    traces = []
    for step in range(1, TM):
        to = lax.rem(tm + step, TM)
        copy = remote(
            dec_v.at[pl.ds(pl.multiple_of(to * 16, 16), 16), :],
            trace_v.at[tm],
            (trace_send.at[step - 1], trace_recv.at[step - 1]),
            (to, chan),
        )
        copy.start()
        traces.append(copy)
    trace_v[tm] = dec_v[pl.ds(pl.multiple_of(tm * 16, 16), 16), :]
    wanted = place_v[pl.ds(pl.multiple_of(x * QUOTA, QUOTA), QUOTA), :]
    slot_lane = lax.broadcasted_iota(jnp.int32, (QUOTA, 128), 1)
    chosen = jnp.concatenate(
        [jnp.where(wanted == slot_lane + part * 128, 1.0, 0.0) for part in range(SLOTS // 128)], axis=1
    ).astype(BF16)
    for copy in spreads:
        copy.wait()
    block_v[...] = dot(chosen, slot_v[...].reshape(SLOTS, 128)).astype(BF16)

    def part_order(buf, axes):
        sizes = {"x": NX, "y": NY, "z": NZ}
        at = {"x": x, "y": y, "z": z}
        order = []
        for number, axis in enumerate(axes):
            lead = [at[a] for a in reversed(axes[number + 1 :])]

            def chunk(index, lead=lead):
                return buf.at[(core, *lead, index)]

            def device(index, axis=axis):
                where = dict(at)
                where[axis] = index
                return place(where["x"], where["y"], where["z"], core)

            order.append((at[axis], sizes[axis], chunk, device))
        return order

    sends = []
    routines = []
    own_copies = []
    bufs = (
        (a_ref, "xyz", a_send, a_recv),
        (b_ref, "yzx", b_send, b_recv),
        (c_ref, "zxy", c_send, c_recv),
        (d_ref, "zxy", d_send, d_recv),
    )
    for number, (buf, axes, send_sem, recv_sem) in enumerate(bufs):
        begin, rows = PARTS[number]
        first = block_v.at[begin : begin + rows]
        at = {"x": x, "y": y, "z": z}
        slot = buf.at[(core, *(at[a] for a in reversed(axes)))]
        copy = pltpu.make_async_copy(first, slot, own_sem.at[number])
        copy.start()
        own_copies.append(copy)
        order = part_order(buf, axes)
        routines.append(gather_part((send_sem, recv_sem), order, direction, sends, first, CUTS[number]))

    twins = []

    def to_twin(block):
        number = len(twins)
        copy = remote(block, block, (twin_send.at[number], twin_recv.at[number]), twin)
        copy.start()
        twins.append(copy)

    def advance(name):
        for block in routines["ABCD".index(name)]:
            if block is None:
                break
            to_twin(block)

    def own_channels(part):
        rows = lax.broadcasted_iota(jnp.int32, (128, HALF), 0)
        alive = lax.rem(rows, 16) < live_ref[0]
        main = trace_v[part * 8 : part * 8 + 8, :, 0:HALF].reshape(128, HALF)
        edges = trace_v[part * 8 : part * 8 + 8, :, HALF:].reshape(128, 128).astype(F32)
        if part:
            before = trace_v[part * 8 - 1, :, HALF:].astype(F32)
        else:
            before = jnp.zeros((16, 128), F32)
        flat = joined(main, edges, jnp.concatenate([before, edges[0:112]], axis=0))
        spec = dot(jnp.where(alive, flat, jnp.zeros_like(flat)), table_v[...])
        for seg in range(NSEG // 2):
            low = spec[seg * 32 : seg * 32 + 16]
            high = spec[seg * 32 + 16 : seg * 32 + 32]
            full = low[:, 0:SEG] + low[:, SEG:] + sign * (high[:, 0:SEG] + high[:, SEG:])
            white = whiten(full).astype(F32)
            for band in range(KG):
                rows_at = pl.ds(part * 4 + seg, 16, stride=NSEG)
                white_ref[band, rows_at, :] = white[:, band * 128 : (band + 1) * 128]

    for name in "ABCD":
        advance(name)
    for copy in own_copies:
        copy.wait()
    for copy in traces:
        copy.wait()
    own_channels(0)
    for number, name in enumerate(ROUNDS):
        if number == 5:
            own_channels(1)
        advance(name)
    for copy in sends:
        copy.wait_send()
    for copy in twins:
        copy.wait()


def correlate_kernel(white_ref, a_ref, b_ref, c_ref, d_ref, lag_ref, out_hbm, all_v, weight_v, cross_v, out_v, out_sem):
    quarter = lax.broadcasted_iota(jnp.int32, (SRC, 128), 1) // 32
    quarter_b = quarter.astype(F32).astype(BF16)

    def merge(blocks, shift, rows=16):
        lanes = (quarter_b if blocks[0].dtype == BF16 else quarter)[0:rows]
        masks = [lanes == j for j in range(4)]
        pieces = []
        for at in range(0, blocks[0].shape[0], rows):
            full = blocks[(0 - shift) % 4][at : at + rows]
            for j in range(1, 4):
                full = jnp.where(masks[j], blocks[(j - shift) % 4][at : at + rows], full)
            pieces.append(full)
        return jnp.concatenate(pieces, axis=0) if len(pieces) > 1 else pieces[0]

    for band in range(KG):
        run, core = band // 2, band % 2
        for four in range(2):
            blocks = []
            for seg in range(four * 4, four * 4 + 4):
                y, z = seg // 2, (seg % 2) * 4 + run
                pieces = []
                for x in range(NX):
                    pieces += [a_ref[core, z, y, x], b_ref[core, x, z, y], c_ref[core, y, x, z], d_ref[core, y, x, z]]
                blocks.append(jnp.concatenate(pieces, axis=0))
            for part in range(QUARTERS):
                lane = ((band * QUARTERS + part) * 2 + four) * 128
                all_v[:, lane : lane + 128] = merge(blocks, part)

    row = lax.broadcasted_iota(jnp.int32, (BINS, 128), 0)
    lane = lax.broadcasted_iota(jnp.int32, (BINS, 128), 1)
    same = row.astype(F32).astype(BF16) == lax.rem(lane, BINS).astype(F32).astype(BF16)

    def spread(rows, seg):
        wide = jnp.broadcast_to(rows[seg : seg + 1], (BINS, 128)).astype(BF16)
        return jnp.where(same, wide, jnp.zeros_like(wide))

    is_re = lax.rem(lane[0:8], 2 * BINS) < BINS

    def copies(which):
        return [
            pltpu.make_async_copy(
                out_v.at[which, part].reshape(SRC, 8, 128),
                out_hbm.at[:, which * 8 : which * 8 + 8, part * 128 : (part + 1) * 128],
                out_sem.at[which, part],
            )
            for part in range(3)
        ]

    @pl.loop(0, 2)
    def _(octet):
        @pl.loop(0, 2)
        def _(band_group):
          for sub in range(4):
            band = band_group * 4 + sub
            crosses = []
            turned = [pltpu.roll(white_ref[band, 8 * octet + c], 32 * (c % 4), 1) if c % 4 else white_ref[band, 8 * octet + c] for c in range(8)]
            for part in range(QUARTERS):
                slot = (sub * QUARTERS + part) % 8
                for group in range(2):
                    v = merge(turned[group * 4 : group * 4 + 4], part, 8)
                    u = jnp.where(is_re, pltpu.roll(v, 128 - BINS, 1), -pltpu.roll(v, BINS, 1))
                    lanes = slice(group * 128, group * 128 + 128)
                    for four in range(2):
                        for j in range(4):
                            seg = four * 4 + (j - part) % 4
                            at = four * 128 + j * 32
                            weight_v[slot, at : at + 16, lanes] = spread(v, seg)
                            weight_v[slot, at + 16 : at + 32, lanes] = spread(u, seg)
                at = pl.multiple_of((band * QUARTERS + part) * 256, 256)
                crosses.append(dot(all_v[:, pl.ds(at, 256)], weight_v[slot]).astype(BF16))
            for c in range(8):
                blocks = [cross[:, c // 4 * 128 : c // 4 * 128 + 128] for cross in crosses]
                full = merge(blocks, c)
                cross_v[c, :, pl.ds(pl.multiple_of(band * 128, 128), 128)] = full
        @pl.loop(0, 2)
        def _(four):
            for c in range(4):
                table = jnp.concatenate(
                    [
                        lag_ref[band * 128 + (j - c) % 4 * 32 : band * 128 + (j - c) % 4 * 32 + 32, :]
                        for band in range(KG)
                        for j in range(4)
                    ],
                    axis=0,
                )
                lags = dot(cross_v[four * 4 + c], table)
                for part in range(3):
                    out_v[octet, part, pl.ds(four * 4 + c, SRC, stride=8), :] = lags[:, part * 128 : (part + 1) * 128]

        for which in range(2):

            @pl.when(octet == which)
            def _():
                for copy in copies(which):
                    copy.start()

    for which in range(2):
        for copy in copies(which):
            copy.wait()


def local(raw_strain, fir_taps, source_channels, live_counts):
    taps = fir_taps[None, :]
    src = source_channels[None, :]
    any_spec = pl.BlockSpec(memory_space=pl.ANY)
    vmem = pl.BlockSpec(memory_space=pltpu.VMEM)
    hbm = pl.BlockSpec(memory_space=pltpu.HBM)
    dma = pltpu.SemaphoreType.DMA
    heights = [rows for _, rows in PARTS]
    early = (NX + NY - 2, NY + NZ - 2, NZ + NX - 2, NZ + NX - 2)
    last = (NZ, NX, NY, NY)
    hops = [start + (size - 1) * cuts for start, size, cuts in zip(early, last, CUTS)]
    blocks = sum(size * cuts for size, cuts in zip(last, CUTS))
    a, b, c, d, white = pl.pallas_call(
        gather_kernel,
        out_shape=(
            pltpu.VMEM((NC, NZ, NY, NX, heights[0], 128), BF16),
            pltpu.VMEM((NC, NX, NZ, NY, heights[1], 128), BF16),
            pltpu.VMEM((NC, NY, NX, NZ, heights[2], 128), BF16),
            pltpu.VMEM((NC, NY, NX, NZ, heights[3], 128), BF16),
            pltpu.VMEM((KG, 16 * NSEG, 128), F32),
        ),
        in_specs=[hbm, vmem, vmem, pl.BlockSpec(memory_space=pltpu.SMEM), hbm],
        out_specs=(vmem, vmem, vmem, vmem, vmem),
        scratch_shapes=[
            pltpu.VMEM((256, 5248), BF16),
            pltpu.VMEM((256, REACH), BF16),
            pltpu.VMEM((256, HALF + 128), BF16),
            pltpu.VMEM((2, 16, HALF + 128), BF16),
            pltpu.VMEM((16, HALF + 128), BF16),
            pltpu.VMEM((2, 16, 128), BF16),
            pltpu.VMEM((TM, 16, HALF + 128), BF16),
            pltpu.VMEM((HALF, 2 * SEG), BF16),
            pltpu.VMEM((KG, 16, 128), BF16),
            pltpu.VMEM((32, 16, 128), BF16),
            pltpu.VMEM((SRC, 128), jnp.int32),
            pltpu.VMEM((QUOTA, 128), BF16),
            dma((4,)),
            dma,
            dma((2, 2)),
            dma((2,)),
            dma((TM - 1,)),
            dma((TM - 1,)),
            *(dma((count,)) for count in hops for _ in range(2)),
            dma((4,)),
            dma((blocks,)),
            dma((blocks,)),
            dma((31,)),
            dma((31,)),
        ],
        compiler_params=pltpu.CompilerParams(
            collective_id=0, has_side_effects=True, vmem_limit_bytes=58 * 1024 * 1024
        ),
        name="filter_and_gather",
    )(raw_strain, taps, src, live_counts, jnp.asarray(dft_table()))
    return pl.pallas_call(
        correlate_kernel,
        out_shape=jax.ShapeDtypeStruct((SRC, 16, 2 * LAGH), F32),
        in_specs=[vmem, vmem, vmem, vmem, vmem, vmem],
        out_specs=any_spec,
        scratch_shapes=[
            pltpu.VMEM((SRC, NSEG * SEG), BF16),
            pltpu.VMEM((8, 256, 256), BF16),
            pltpu.VMEM((8, SRC, SEG), BF16),
            pltpu.VMEM((2, 3, SRC * 8, 128), F32),
            dma((2, 3)),
        ],
        compiler_params=pltpu.CompilerParams(vmem_limit_bytes=36 * 1024 * 1024),
        name="correlate",
    )(white.reshape(KG, 16, NSEG, 128), a, b, c, d, jnp.asarray(lag_table()))


def solution(mesh):
    placed = (P("chan", "tm"), P(), P(), P(("chan", "tm")))
    return jax.shard_map(
        local, mesh=mesh, in_specs=placed, out_specs=P(None, ("chan", "tm"), None), check_vma=False
    )
```

```python
import functools
import math

import jax
import jax.numpy as jnp
import numpy as np
from jax import lax
from jax.experimental import pallas as pl
from jax.experimental.pallas import tpu as pltpu
from jax.sharding import PartitionSpec as P

NX, NY, NZ, NC = 4, 4, 8, 2
TM, CHAN = 16, 16
DECIM, SEG, BAND, LAGH = 10, 1024, 64, 192
NSEG = 8
HALF = SEG // 2
SRC = 256
SLOTS = 512
EPS = 1e-06
MESH = pl.DeviceIdType.MESH
F32, BF16 = jnp.float32, jnp.bfloat16
TAPS = 128
REACH = 1408
KG = HALF // BAND
EDGE = 16
QUARTERS, BINS = 4, 16
QUOTA = SRC // NX
PARTS = ((0, 16), (16, 16), (32, 16), (48, 16))
ROUNDS = "ABCDACDBAAAACBADAAABCDAAABACBCADAAAD"
CUTS = (4, 2, 2, 2)


def dot(a, b):
    return jnp.dot(a, b, preferred_element_type=F32)


def hi_lo(table):
    hi = table.astype(np.float32).astype(jnp.bfloat16)
    lo = (table - hi.astype(np.float64)).astype(np.float32).astype(jnp.bfloat16)
    return hi, lo


def dft_table():
    n = np.arange(HALF)[:, None]
    k = np.arange(HALF)[None, :]
    phase = (n * k % SEG) * (2.0 * np.pi / SEG)
    both = np.stack([np.cos(phase), -np.sin(phase)], axis=1).reshape(HALF, 2, KG, QUARTERS, BINS)
    table = both.transpose(0, 2, 3, 1, 4).reshape(HALF, SEG)
    return np.concatenate(hi_lo(table), axis=1)


def lag_table():
    k = np.arange(HALF)[:, None]
    t = np.arange(-LAGH, LAGH)[None, :]
    phase = (k * t % SEG) * (2.0 * np.pi / SEG)
    weight = np.where(k == 0, 1.0, 2.0) * (math.sqrt(SEG / NSEG) / SEG)
    both = np.stack([weight * np.cos(phase), -weight * np.sin(phase)], axis=0)
    table = both.reshape(2, KG, QUARTERS, BINS, 2 * LAGH).transpose(1, 2, 0, 3, 4).reshape(SEG, 2 * LAGH)
    return table.astype(np.float32).astype(jnp.bfloat16)


def whiten(spec, turn=None):
    bands = []
    for band in range(KG):
        block = spec[:, band * 128 : (band + 1) * 128]
        power = jnp.sum(block * block, axis=1, keepdims=True) * (1.0 / BAND)
        block = block * lax.rsqrt(power + EPS)
        bands.append(block if turn is None else pltpu.roll(block, turn, 1))
    return jnp.concatenate(bands, axis=1).astype(BF16)


def odd_sign(rows):
    lane = lax.broadcasted_iota(jnp.int32, (rows, SEG), 1)
    return (1 - 2 * lax.rem(lane, 2)).astype(F32)


def place(x, y, z, core):
    return (y * 4 + z // 2, lax.rem(z, 2) * 8 + x * 2 + core)


def gather_part(semaphores, order, step_dir, sends, first, cuts):
    send_sem, recv_sem = semaphores
    count = 0
    for stage, (me, size, chunk, device) in enumerate(order):

        def index(offset):
            return lax.rem(me + step_dir * offset + size, size)

        def copy_of(src, to, number):
            return pltpu.make_async_remote_copy(
                src_ref=src[0],
                dst_ref=src[1],
                send_sem=send_sem.at[number],
                recv_sem=recv_sem.at[number],
                device_id=device(index(to)),
                device_id_type=MESH,
            )

        def send(src, dst, to, number):
            copy = copy_of((src, dst), to, number)
            copy.start()
            sends.append(copy)

        def arrived(offset, number):
            block = chunk(index(offset))
            copy_of((block, block), 1, number).wait_recv()
            return block

        own = chunk(me)
        start = first if stage == 0 else own
        if stage < len(order) - 1:
            for offset in range(1, size):
                send(start, own, offset, count + offset - 1)
            yield None
            for offset in range(1, size):
                arrived(-offset, count + offset - 1)
            count += size - 1
            continue
        far, near = size // 2, size - 1 - size // 2

        def piece(index, cut):
            block = chunk(index)
            depth = block.shape[0] // cuts
            return block.at[cut * depth : (cut + 1) * depth]

        def arrived_piece(offset, number, cut):
            block = piece(index(offset), cut)
            copy_of((block, block), 1, number).wait_recv()
            return block

        def number_of(hop, cut):
            return count + hop * cuts + cut

        for cut in range(cuts):
            own = piece(me, cut)
            send(own, own, 1, number_of(0, cut))
            send(own, own, -1, number_of(far, cut))
        for cut in range(cuts):
            yield piece(me, cut)
        for hop in range(1, far + 1):
            for cut in range(cuts):
                yield None
                block = arrived_piece(-hop, number_of(hop - 1, cut), cut)
                if hop < far:
                    send(block, block, 1, number_of(hop, cut))
                yield block
                if hop <= near:
                    block = arrived_piece(hop, number_of(far + hop - 1, cut), cut)
                    if hop < near:
                        send(block, block, -1, number_of(far + hop, cut))
                    yield block


def gather_kernel(
    raw_hbm, taps_ref, src_ref, live_ref, table_hbm,
    a_ref, b_ref, c_ref, d_ref, white_ref,
    raw_v, tap_v, dec_v, sel_v, pair_v, edge_v, trace_v, table_v, own_v, slot_v, place_v, block_v,
    load_sem, table_sem, halo_sem, pair_sem, trace_send, trace_recv,
    a_send, a_recv, b_send, b_recv, c_send, c_recv, d_send, d_recv, own_sem, twin_send, twin_recv, spread_send, spread_recv,
):
    tm = lax.axis_index("tm")
    chan = lax.axis_index("chan")
    y, z_hi = tm // 4, lax.rem(tm, 4)
    z_lo, x, core = chan // 8, lax.rem(chan, 8) // 2, lax.rem(chan, 2)
    z = z_hi * 2 + z_lo
    direction = 1 - 2 * core
    half = lax.rem(tm, 2)

    def remote(src, dst, sems, device):
        return pltpu.make_async_remote_copy(
            src_ref=src, dst_ref=dst, send_sem=sems[0], recv_sem=sems[1], device_id=device, device_id_type=MESH
        )

    loads = []
    for part in range(4):
        loads.append(
            pltpu.make_async_copy(
                raw_hbm.at[:, part * 1280 : (part + 1) * 1280],
                raw_v.at[:, 128 + part * 1280 : 128 + (part + 1) * 1280],
                load_sem.at[part],
            )
        )
        loads[-1].start()
    table_load = pltpu.make_async_copy(table_hbm, table_v, table_sem)
    table_load.start()

    barrier = pltpu.get_barrier_semaphore()
    peers = [(lax.rem(tm + step, TM), chan) for step in range(1, TM)]
    twin = place(x, y, z, 1 - core)
    run = lax.rem(z, 4)
    spread = []
    for step in range(1, 32):
        to_run = lax.rem(run + step // 8, 4)
        to_x = lax.rem(x + step // 2, NX)
        to_core = lax.rem(core + step, NC)
        spread.append((place(to_x, y, z - run + to_run, to_core), to_run * 2 + to_core))
        peers.append(spread[-1][0])
    for step in (1, 3, 5, 7):
        peers.append(place(x, y, lax.rem(z + step, NZ), core))
    for peer in peers:
        pl.semaphore_signal(barrier, inc=1, device_id=peer, device_id_type=MESH)
    taps_col = jnp.transpose(jnp.broadcast_to(taps_ref[...], (TAPS, TAPS)))
    tap_row = lax.broadcasted_iota(jnp.int32, (TAPS, 384), 0)
    tap_lane = lax.broadcasted_iota(jnp.int32, (TAPS, 384), 1)
    taps_wide = jnp.concatenate([taps_col] * 3, axis=1)
    rev = jnp.sum(jnp.where(tap_row + tap_lane == TAPS, taps_wide, 0.0), axis=0, keepdims=True)
    base = pltpu.roll(jnp.broadcast_to(rev, (8, 384)), 0, 1, stride=DECIM, stride_axis=0)
    for group in range(8):
        rows = []
        for octet in (2 * group, 2 * group + 1):
            at, turn = divmod(octet * 8 * DECIM, 128)
            piece = pltpu.roll(base, turn, 1) if turn else base
            blocks = [jnp.zeros((8, 128), F32)] * (REACH // 128)
            for number in range(min(3, REACH // 128 - at)):
                blocks[at + number] = piece[:, number * 128 : (number + 1) * 128]
            rows.append(jnp.concatenate(blocks, axis=1))
        band = jnp.concatenate(rows, axis=0)
        band_hi = band.astype(BF16)
        tap_v[group * 16 : group * 16 + 16, :] = band_hi
        tap_v[128 + group * 16 : 128 + group * 16 + 16, :] = (band - band_hi.astype(F32)).astype(BF16)

    src = src_ref[...].astype(F32)
    src_col = jnp.transpose(jnp.broadcast_to(src, (SRC, SRC)))
    lane = lax.broadcasted_iota(jnp.int32, (SRC, SRC), 1)
    row = lax.broadcasted_iota(jnp.int32, (SRC, SRC), 0)
    hit = jnp.where(src_col == (lane + chan * 256).astype(F32), 1.0, 0.0)
    is_src = jnp.sum(hit, axis=0, keepdims=True)
    earlier = jnp.where((row // 16 == lane // 16) & (row < lane), 1.0, 0.0)
    rank = dot(jnp.broadcast_to(is_src, (16, SRC)).astype(BF16), earlier.astype(BF16))[0:1, :]
    pick_row = lax.broadcasted_iota(jnp.int32, (32, SRC), 0)
    pick_lane = lax.broadcasted_iota(jnp.int32, (32, SRC), 1)
    pick = jnp.where(
        (pick_row // 2 == pick_lane // 16) & (lax.rem(pick_row, 2).astype(F32) == rank) & (is_src > 0.5), 1.0, 0.0
    ).astype(BF16)

    src_row = jnp.broadcast_to(src, (SRC, SRC))
    row_block = jnp.floor(src_row * (1.0 / 16))
    col_block = jnp.floor(src_col * (1.0 / 16))
    before = jnp.where((row_block == col_block) & (src_row < src_col), 1.0, 0.0)
    behind = jnp.sum(before, axis=1, keepdims=True).astype(jnp.int32)
    block_of = col_block[:, 0:1].astype(jnp.int32)
    chan_of, local_of = block_of // 16, lax.rem(block_of, 16)
    spot = ((local_of // 8) * 2 + chan_of // 8) * 128 + lax.rem(chan_of, 8) * 16 + 2 * lax.rem(local_of, 8) + behind
    place_v[...] = jnp.broadcast_to(spot, (SRC, 128))

    def filtered(samples, taps):
        both = lax.dot_general(samples, taps, (((1,), (1,)), ((), ())), preferred_element_type=F32)
        return both[:, 0:128] + both[:, 128:256]

    raw_v[:, 0:128] = jnp.zeros((256, 128), BF16)
    heads = None
    for part in range(4):
        loads[part].wait()
        sums = filtered(raw_v[:, part * 1280 : part * 1280 + REACH], tap_v[...])
        dec_v[:, part * 128 : (part + 1) * 128] = sums.astype(BF16)
        heads = sums if part == 0 else heads
    tails = filtered(raw_v[:, 5120:5248], tap_v[:, 0:128])
    edge_lane = lax.broadcasted_iota(jnp.int32, (256, 128), 1)
    edge = jnp.where(edge_lane < 64, heads, pltpu.roll(tails, 64, 1))
    edge = jnp.where(lax.rem(edge_lane, 64) < EDGE, edge, 0.0)
    packed = jnp.zeros((256, 128), F32)
    for number in range(3):
        piece = edge.astype(BF16).astype(F32)
        edge = edge - piece
        packed = packed + (pltpu.roll(piece, number * EDGE, 1) if number else piece)
    dec_v[:, HALF:] = packed.astype(BF16)

    def joined(main, edges, before):
        def whole(rows, at):
            full = pltpu.roll(rows, 128 - at, 1) if at else rows
            for number in (1, 2):
                full = full + pltpu.roll(rows, 128 - at - number * EDGE, 1)
            return full

        sums = (whole(edges.astype(F32), 0) + whole(before.astype(F32), 64)).astype(BF16)
        lanes = lax.broadcasted_iota(jnp.int32, sums.shape, 1)
        first = jnp.where(lanes < EDGE, sums.astype(F32), main[:, 0:128].astype(F32)).astype(BF16)
        return jnp.concatenate([first, main[:, 128:]], axis=1)

    picked = dot(pick, dec_v[...]).astype(BF16)
    sel_v[0] = picked[0:16]
    sel_v[1] = picked[16:32]
    pl.semaphore_wait(barrier, len(peers))
    pair = remote(sel_v.at[1 - half], pair_v, (pair_sem.at[0], pair_sem.at[1]), (tm + 1 - 2 * half, chan))
    pair.start()
    edge_copies = []
    for step in (1, 2):
        copy = remote(
            sel_v.at[(1 - half) if step == 1 else half, :, HALF:],
            edge_v.at[step - 1],
            (halo_sem.at[0, step - 1], halo_sem.at[1, step - 1]),
            (lax.rem(tm + step, TM), chan),
        )
        copy.start()
        edge_copies.append(copy)

    pair.wait()
    for copy in edge_copies:
        copy.wait()
    table_load.wait()
    is_first = half == 0
    mine, other = sel_v[half].astype(F32), pair_v[...].astype(F32)
    low, high = jnp.where(is_first, mine, other), jnp.where(is_first, other, mine)
    tail = jnp.where(is_first, edge_v[0].astype(F32), edge_v[1].astype(F32))
    tail = jnp.where(tm // 2 == 0, 0.0, tail)
    low_edge, high_edge = low[:, HALF:], high[:, HALF:]
    low = joined(low[:, 0:HALF].astype(BF16), low_edge, tail)
    high = joined(high[:, 0:HALF].astype(BF16), high_edge, low_edge)
    spec = dot(jnp.concatenate([low, high], axis=0), table_v[...])
    sign = odd_sign(16)
    full = whiten(
        spec[0:16, 0:SEG] + spec[0:16, SEG:] + sign * (spec[16:32, 0:SEG] + spec[16:32, SEG:]),
        32 * lax.rem(tm // 2, 4),
    )
    for band in range(KG):
        own_v[band] = full[:, band * 128 : (band + 1) * 128]

    here = run * 8 + x * 2 + core
    spreads = []
    for number, (peer, band) in enumerate(spread):
        copy = remote(own_v.at[band], slot_v.at[here], (spread_send.at[number], spread_recv.at[number]), peer)
        copy.start()
        spreads.append(copy)
    slot_v[here] = own_v[run * 2 + core]

    traces = []
    for step in range(1, TM):
        to = lax.rem(tm + step, TM)
        copy = remote(
            dec_v.at[pl.ds(pl.multiple_of(to * 16, 16), 16), :],
            trace_v.at[tm],
            (trace_send.at[step - 1], trace_recv.at[step - 1]),
            (to, chan),
        )
        copy.start()
        traces.append(copy)
    trace_v[tm] = dec_v[pl.ds(pl.multiple_of(tm * 16, 16), 16), :]
    wanted = place_v[pl.ds(pl.multiple_of(x * QUOTA, QUOTA), QUOTA), :]
    slot_lane = lax.broadcasted_iota(jnp.int32, (QUOTA, 128), 1)
    chosen = jnp.concatenate(
        [jnp.where(wanted == slot_lane + part * 128, 1.0, 0.0) for part in range(SLOTS // 128)], axis=1
    ).astype(BF16)
    for copy in spreads:
        copy.wait()
    block_v[...] = dot(chosen, slot_v[...].reshape(SLOTS, 128)).astype(BF16)

    def part_order(buf, axes):
        sizes = {"x": NX, "y": NY, "z": NZ}
        at = {"x": x, "y": y, "z": z}
        order = []
        for number, axis in enumerate(axes):
            lead = [at[a] for a in reversed(axes[number + 1 :])]

            def chunk(index, lead=lead):
                return buf.at[(core, *lead, index)]

            def device(index, axis=axis):
                where = dict(at)
                where[axis] = index
                return place(where["x"], where["y"], where["z"], core)

            order.append((at[axis], sizes[axis], chunk, device))
        return order

    sends = []
    routines = []
    own_copies = []
    bufs = (
        (a_ref, "xyz", a_send, a_recv),
        (b_ref, "yzx", b_send, b_recv),
        (c_ref, "zxy", c_send, c_recv),
        (d_ref, "zxy", d_send, d_recv),
    )
    for number, (buf, axes, send_sem, recv_sem) in enumerate(bufs):
        begin, rows = PARTS[number]
        first = block_v.at[begin : begin + rows]
        at = {"x": x, "y": y, "z": z}
        slot = buf.at[(core, *(at[a] for a in reversed(axes)))]
        copy = pltpu.make_async_copy(first, slot, own_sem.at[number])
        copy.start()
        own_copies.append(copy)
        order = part_order(buf, axes)
        routines.append(gather_part((send_sem, recv_sem), order, direction, sends, first, CUTS[number]))

    twins = []

    def to_twin(block):
        number = len(twins)
        copy = remote(block, block, (twin_send.at[number], twin_recv.at[number]), twin)
        copy.start()
        twins.append(copy)

    def advance(name):
        for block in routines["ABCD".index(name)]:
            if block is None:
                break
            to_twin(block)

    def own_channels(part):
        rows = lax.broadcasted_iota(jnp.int32, (128, HALF), 0)
        alive = lax.rem(rows, 16) < live_ref[0]
        main = trace_v[part * 8 : part * 8 + 8, :, 0:HALF].reshape(128, HALF)
        edges = trace_v[part * 8 : part * 8 + 8, :, HALF:].reshape(128, 128).astype(F32)
        if part:
            before = trace_v[part * 8 - 1, :, HALF:].astype(F32)
        else:
            before = jnp.zeros((16, 128), F32)
        flat = joined(main, edges, jnp.concatenate([before, edges[0:112]], axis=0))
        spec = dot(jnp.where(alive, flat, jnp.zeros_like(flat)), table_v[...])
        for seg in range(NSEG // 2):
            low = spec[seg * 32 : seg * 32 + 16]
            high = spec[seg * 32 + 16 : seg * 32 + 32]
            full = low[:, 0:SEG] + low[:, SEG:] + sign * (high[:, 0:SEG] + high[:, SEG:])
            white = whiten(full).astype(F32)
            for band in range(KG):
                rows_at = pl.ds(part * 4 + seg, 16, stride=NSEG)
                white_ref[band, rows_at, :] = white[:, band * 128 : (band + 1) * 128]

    for name in "ABCD":
        advance(name)
    for copy in own_copies:
        copy.wait()
    for copy in traces:
        copy.wait()
    own_channels(0)
    for number, name in enumerate(ROUNDS):
        if number == 5:
            own_channels(1)
        advance(name)
    for copy in sends:
        copy.wait_send()
    for copy in twins:
        copy.wait()


def correlate_kernel(white_ref, a_ref, b_ref, c_ref, d_ref, lag_ref, out_hbm, all_v, weight_v, cross_v, out_v, out_sem):
    quarter = lax.broadcasted_iota(jnp.int32, (SRC, 128), 1) // 32
    quarter_b = quarter.astype(F32).astype(BF16)

    def merge(blocks, shift, rows=16):
        lanes = (quarter_b if blocks[0].dtype == BF16 else quarter)[0:rows]
        masks = [lanes == j for j in range(4)]
        pieces = []
        for at in range(0, blocks[0].shape[0], rows):
            full = blocks[(0 - shift) % 4][at : at + rows]
            for j in range(1, 4):
                full = jnp.where(masks[j], blocks[(j - shift) % 4][at : at + rows], full)
            pieces.append(full)
        return jnp.concatenate(pieces, axis=0) if len(pieces) > 1 else pieces[0]

    for band in range(KG):
        run, core = band // 2, band % 2
        for four in range(2):
            blocks = []
            for seg in range(four * 4, four * 4 + 4):
                y, z = seg // 2, (seg % 2) * 4 + run
                pieces = []
                for x in range(NX):
                    pieces += [a_ref[core, z, y, x], b_ref[core, x, z, y], c_ref[core, y, x, z], d_ref[core, y, x, z]]
                blocks.append(jnp.concatenate(pieces, axis=0))
            for part in range(QUARTERS):
                lane = ((band * QUARTERS + part) * 2 + four) * 128
                all_v[:, lane : lane + 128] = merge(blocks, part)

    row = lax.broadcasted_iota(jnp.int32, (BINS, 128), 0)
    lane = lax.broadcasted_iota(jnp.int32, (BINS, 128), 1)
    same = row.astype(F32).astype(BF16) == lax.rem(lane, BINS).astype(F32).astype(BF16)

    def spread(rows, seg):
        wide = jnp.broadcast_to(rows[seg : seg + 1], (BINS, 128)).astype(BF16)
        return jnp.where(same, wide, jnp.zeros_like(wide))

    is_re = lax.rem(lane[0:8], 2 * BINS) < BINS

    def copies(which):
        return [
            pltpu.make_async_copy(
                out_v.at[which, part].reshape(SRC, 8, 128),
                out_hbm.at[:, which * 8 : which * 8 + 8, part * 128 : (part + 1) * 128],
                out_sem.at[which, part],
            )
            for part in range(3)
        ]

    @pl.loop(0, 2)
    def _(octet):
        @pl.loop(0, 2)
        def _(band_group):
          for sub in range(4):
            band = band_group * 4 + sub
            crosses = []
            turned = [pltpu.roll(white_ref[band, 8 * octet + c], 32 * (c % 4), 1) if c % 4 else white_ref[band, 8 * octet + c] for c in range(8)]
            for part in range(QUARTERS):
                slot = (sub * QUARTERS + part) % 8
                for group in range(2):
                    v = merge(turned[group * 4 : group * 4 + 4], part, 8)
                    u = jnp.where(is_re, pltpu.roll(v, 128 - BINS, 1), -pltpu.roll(v, BINS, 1))
                    lanes = slice(group * 128, group * 128 + 128)
                    for four in range(2):
                        for j in range(4):
                            seg = four * 4 + (j - part) % 4
                            at = four * 128 + j * 32
                            weight_v[slot, at : at + 16, lanes] = spread(v, seg)
                            weight_v[slot, at + 16 : at + 32, lanes] = spread(u, seg)
                at = pl.multiple_of((band * QUARTERS + part) * 256, 256)
                crosses.append(dot(all_v[:, pl.ds(at, 256)], weight_v[slot]).astype(BF16))
            for c in range(8):
                blocks = [cross[:, c // 4 * 128 : c // 4 * 128 + 128] for cross in crosses]
                full = merge(blocks, c)
                cross_v[c, :, pl.ds(pl.multiple_of(band * 128, 128), 128)] = full
        @pl.loop(0, 2)
        def _(four):
            for c in range(4):
                table = jnp.concatenate(
                    [
                        lag_ref[band * 128 + (j - c) % 4 * 32 : band * 128 + (j - c) % 4 * 32 + 32, :]
                        for band in range(KG)
                        for j in range(4)
                    ],
                    axis=0,
                )
                lags = dot(cross_v[four * 4 + c], table)
                for part in range(3):
                    out_v[octet, part, pl.ds(four * 4 + c, SRC, stride=8), :] = lags[:, part * 128 : (part + 1) * 128]

        for which in range(2):

            @pl.when(octet == which)
            def _():
                for copy in copies(which):
                    copy.start()

    for which in range(2):
        for copy in copies(which):
            copy.wait()


def local(raw_strain, fir_taps, source_channels, live_counts):
    taps = fir_taps[None, :]
    src = source_channels[None, :]
    any_spec = pl.BlockSpec(memory_space=pl.ANY)
    vmem = pl.BlockSpec(memory_space=pltpu.VMEM)
    hbm = pl.BlockSpec(memory_space=pltpu.HBM)
    dma = pltpu.SemaphoreType.DMA
    heights = [rows for _, rows in PARTS]
    early = (NX + NY - 2, NY + NZ - 2, NZ + NX - 2, NZ + NX - 2)
    last = (NZ, NX, NY, NY)
    hops = [start + (size - 1) * cuts for start, size, cuts in zip(early, last, CUTS)]
    blocks = sum(size * cuts for size, cuts in zip(last, CUTS))
    a, b, c, d, white = pl.pallas_call(
        gather_kernel,
        out_shape=(
            pltpu.VMEM((NC, NZ, NY, NX, heights[0], 128), BF16),
            pltpu.VMEM((NC, NX, NZ, NY, heights[1], 128), BF16),
            pltpu.VMEM((NC, NY, NX, NZ, heights[2], 128), BF16),
            pltpu.VMEM((NC, NY, NX, NZ, heights[3], 128), BF16),
            pltpu.VMEM((KG, 16 * NSEG, 128), F32),
        ),
        in_specs=[hbm, vmem, vmem, pl.BlockSpec(memory_space=pltpu.SMEM), hbm],
        out_specs=(vmem, vmem, vmem, vmem, vmem),
        scratch_shapes=[
            pltpu.VMEM((256, 5248), BF16),
            pltpu.VMEM((256, REACH), BF16),
            pltpu.VMEM((256, HALF + 128), BF16),
            pltpu.VMEM((2, 16, HALF + 128), BF16),
            pltpu.VMEM((16, HALF + 128), BF16),
            pltpu.VMEM((2, 16, 128), BF16),
            pltpu.VMEM((TM, 16, HALF + 128), BF16),
            pltpu.VMEM((HALF, 2 * SEG), BF16),
            pltpu.VMEM((KG, 16, 128), BF16),
            pltpu.VMEM((32, 16, 128), BF16),
            pltpu.VMEM((SRC, 128), jnp.int32),
            pltpu.VMEM((QUOTA, 128), BF16),
            dma((4,)),
            dma,
            dma((2, 2)),
            dma((2,)),
            dma((TM - 1,)),
            dma((TM - 1,)),
            *(dma((count,)) for count in hops for _ in range(2)),
            dma((4,)),
            dma((blocks,)),
            dma((blocks,)),
            dma((31,)),
            dma((31,)),
        ],
        compiler_params=pltpu.CompilerParams(
            collective_id=0, has_side_effects=True, vmem_limit_bytes=58 * 1024 * 1024
        ),
        name="filter_and_gather",
    )(raw_strain, taps, src, live_counts, jnp.asarray(dft_table()))
    return pl.pallas_call(
        correlate_kernel,
        out_shape=jax.ShapeDtypeStruct((SRC, 16, 2 * LAGH), F32),
        in_specs=[vmem, vmem, vmem, vmem, vmem, vmem],
        out_specs=any_spec,
        scratch_shapes=[
            pltpu.VMEM((SRC, NSEG * SEG), BF16),
            pltpu.VMEM((8, 256, 256), BF16),
            pltpu.VMEM((8, SRC, SEG), BF16),
            pltpu.VMEM((2, 3, SRC * 8, 128), F32),
            dma((2, 3)),
        ],
        compiler_params=pltpu.CompilerParams(vmem_limit_bytes=36 * 1024 * 1024),
        name="correlate",
    )(white.reshape(KG, 16, NSEG, 128), a, b, c, d, jnp.asarray(lag_table()))


def solution(mesh):
    placed = (P("chan", "tm"), P(), P(), P(("chan", "tm")))
    return jax.shard_map(
        local, mesh=mesh, in_specs=placed, out_specs=P(None, ("chan", "tm"), None), check_vma=False
    )
```
